512 devices in a mesh: dp: 64 (over z, y), expert: 8 (over x, core).
Axes of the slice: x: 4, y: 4, z: 16, core: 2. Of those that a mesh axis runs over, the one named last changes fastest.
Arguments:
- attn_input: bfloat16 [16384, 7168], P('dp', 'expert'), may hold values from -6 to 6
- latent_grad: bfloat16 [16384, 512], P('dp'), may hold values from -0.046875 to 0.046875
- latent_param: float32 [8, 896, 512], P('expert', 'dp'), may hold values from -6 to 6
- latent_first: float32 [8, 896, 512], P('expert', 'dp'), may hold values from -3 to 3
- latent_second: float32 [8, 896, 512], P('expert', 'dp'), may hold values from 0.05 to 1
- expert_input: bfloat16 [8, 5632, 7168], P('expert', 'dp'), may hold values from -6 to 6
- hidden_grad: bfloat16 [8, 5632, 1024], P('expert', 'dp'), may hold values from -0.109375 to 0.109375
- counts: int32 [64, 8], replicated, may hold values from 0 to 88, as said below
- block_owner: int32 [8, 64], P('expert'), may hold values from 0 to 63, each once within a row
- expert_param: float32 [8, 7168, 1024], P('expert', 'dp'), may hold values from -6 to 6
- expert_first: float32 [8, 7168, 1024], P('expert', 'dp'), may hold values from -3 to 3
- expert_second: float32 [8, 7168, 1024], P('expert', 'dp'), may hold values from 0.05 to 1
Outputs:
- latent_param_new: float32 [8, 896, 512], P('expert', 'dp')
- latent_first_new: float32 [8, 896, 512], P('expert', 'dp')
- latent_second_new: float32 [8, 896, 512], P('expert', 'dp')
- expert_param_new: float32 [8, 7168, 1024], P('expert', 'dp')
- expert_first_new: float32 [8, 7168, 1024], P('expert', 'dp')
- expert_second_new: float32 [8, 7168, 1024], P('expert', 'dp')
The draws below stay inside these ranges and needn't reach their ends.
Inputs may be any that keep to these rules, and one draw needn't show every extreme that they name: The live rows of an expert on a dp index fill its first slots. For each aligned pair of dp indices 2m and 2m + 1 the two counts of an expert sum to at most 88; for every expert some pair sums to exactly 88 and some dp index holds exactly 88. Each row is a permutation: block b of 112 rows of expert e is updated by dp index block_owner[e, b].
All inputs are finite; a program needn't handle non-finite values.
Results may differ from the reference program's by a relative error of at most 0.0003.
Values may be sent and summed in bfloat16 or wider, within the bound.
A program may use at most 64 MiB of HBM per device.

```python
import math
import jax
import jax.numpy as jnp
from jax import lax

SHARD = 112
LAT = 512
FFE = 1024
CAP = 88
STEP = 20
D = 7168
SLICES = 8
FEAT = 896
EXPERTS = 8
SLOTS = 5632
TOKENS = 16384
N_DP = 64


def draw_counts(key, part):
    pair_count = N_DP // 2
    key_total = jax.random.fold_in(key, 11)
    key_split = jax.random.fold_in(key, 12)
    key_chosen = jax.random.fold_in(key, 13)
    key_side = jax.random.fold_in(key, 14)
    totals = jax.random.randint(key_total, (pair_count, EXPERTS), 3 * CAP // 5, CAP + 1)
    lower_part = jax.random.randint(key_split, (pair_count, EXPERTS), 0, totals + 1)
    chosen = jax.random.randint(key_chosen, (1, EXPERTS), 0, pair_count)
    side_bit = jax.random.randint(key_side, (1, EXPERTS), 0, 2)
    pair_rows = jnp.arange(pair_count, dtype=jnp.int32)[:, None]
    forced = pair_rows == chosen
    totals = jnp.where(forced, CAP, totals)
    lower_part = jnp.where(forced, CAP * (1 - side_bit), lower_part)
    upper_part = totals - lower_part
    stacked = jnp.stack([lower_part, upper_part], axis=1)
    return stacked.reshape(N_DP, EXPERTS).astype(jnp.int32)


def steps_of(rng, shape, pieces, low, high):
    def one(axis_at, shards_of):
        steps = jax.random.uniform(jax.random.fold_in(jax.random.fold_in(rng, 6), axis_at), (shards_of,), jnp.float32, low / len(pieces), high / len(pieces))
        return jnp.repeat(jnp.exp(steps), shape[axis_at] // shards_of).reshape((-1,) + (1,) * (len(shape) - axis_at - 1))

    factor_of = one(*pieces[0])
    for cut in pieces[1:]:
        factor_of = factor_of * one(*cut)
    return factor_of


def noise(own_key, shape, width, most, split=(), kind=jnp.bfloat16):
    drawn = width * jax.random.normal(own_key, shape, jnp.float32)
    if split:
        drawn = drawn * steps_of(own_key, shape, split, -0.22, 0.18)
    return jnp.clip(drawn, -most, most).astype(kind)


def setup_inputs(seed: int = 0) -> dict:
    key_of = jax.random.split(jax.random.key(seed), 13)
    attn_input = noise(key_of[0], (TOKENS, D), 1.0, 6.0, ((0, 64), (1, 8)))
    latent_grad = noise(key_of[1], (TOKENS, LAT), TOKENS ** -0.5, 0.046875, ((0, 64),))
    latent_param = noise(key_of[2], (SLICES, FEAT, LAT), 1.0, 6.0, ((0, 8), (1, 64)), jnp.float32)
    latent_first = noise(key_of[3], (SLICES, FEAT, LAT), 0.5, 3.0, ((0, 8), (1, 64)), jnp.float32)
    latent_second = jnp.clip(jnp.exp(math.log(1.0) - 2.9957323 * jax.random.uniform(key_of[4], (SLICES, FEAT, LAT), jnp.float32) ** steps_of(key_of[4], (SLICES, FEAT, LAT), ((0, 8), (1, 64)), -0.2, 0.2)), 0.05, 1.0)
    expert_input = noise(key_of[5], (EXPERTS, SLOTS, D), 1.0, 6.0, ((0, 8), (1, 64)))
    hidden_grad = noise(key_of[6], (EXPERTS, SLOTS, FFE), (CAP * N_DP // 2) ** -0.5, 0.109375, ((0, 8), (1, 64)))
    counts = draw_counts(jax.random.fold_in(key_of[12], 71), 0)
    block_owner = jax.vmap(lambda own: jax.random.permutation(own, N_DP))(jax.random.split(key_of[8], EXPERTS)).reshape((EXPERTS, N_DP)).astype(jnp.int32)
    expert_param = noise(key_of[9], (EXPERTS, D, FFE), 1.0, 6.0, ((0, 8), (1, 64)), jnp.float32)
    expert_first = noise(key_of[10], (EXPERTS, D, FFE), 0.5, 3.0, ((0, 8), (1, 64)), jnp.float32)
    expert_second = jnp.clip(jnp.exp(math.log(1.0) - 2.9957323 * jax.random.uniform(key_of[11], (EXPERTS, D, FFE), jnp.float32) ** steps_of(key_of[11], (EXPERTS, D, FFE), ((0, 8), (1, 64)), -0.2, 0.2)), 0.05, 1.0)
    return dict(attn_input=attn_input, latent_grad=latent_grad, latent_param=latent_param, latent_first=latent_first, latent_second=latent_second, expert_input=expert_input, hidden_grad=hidden_grad, counts=counts, block_owner=block_owner, expert_param=expert_param, expert_first=expert_first, expert_second=expert_second)


FIRST_BETA = 0.9
SECOND_BETA = 0.95
LEARNING_RATE = 0.1
WEIGHT_DECAY = 0.5
EPSILON = 1e-08

def adam_step(gradient, weights, moment_one, moment_two):
    first_new = FIRST_BETA * moment_one + (1.0 - FIRST_BETA) * gradient
    second_new = SECOND_BETA * moment_two + (1.0 - SECOND_BETA) * gradient * gradient
    mean_hat = first_new / (1.0 - FIRST_BETA ** STEP)
    scale_hat = second_new / (1.0 - SECOND_BETA ** STEP)
    update = mean_hat / (jnp.sqrt(scale_hat) + EPSILON) + WEIGHT_DECAY * weights
    return (weights - LEARNING_RATE * update, first_new, second_new)

def reference(attn_input, latent_grad, latent_param, latent_first, latent_second, expert_input, hidden_grad, counts, block_owner, expert_param, expert_first, expert_second):
    grad_latent = lax.dot_general(attn_input, latent_grad, (((0,), (0,)), ((), ())), preferred_element_type=jnp.float32)
    grad_latent = grad_latent.reshape(SLICES, FEAT, LAT)
    latent_new = adam_step(grad_latent, latent_param, latent_first, latent_second)
    slot_index = jnp.arange(SLOTS, dtype=jnp.int32)

    def one_expert(operands):
        inputs, hidden, count_col, owners = operands
        limits = jnp.repeat(count_col, CAP, total_repeat_length=SLOTS)
        live = slot_index % CAP < limits
        masked = jnp.where(live[:, None], inputs, jnp.zeros_like(inputs))
        gradient = lax.dot_general(masked, hidden, (((0,), (0,)), ((), ())), preferred_element_type=jnp.float32)
        blocks = gradient.reshape(N_DP, SHARD, FFE)
        owned = jnp.zeros_like(blocks).at[owners].set(blocks)
        return owned.reshape(D, FFE)
    grad_expert = lax.map(one_expert, (expert_input, hidden_grad, counts.T.astype(jnp.int32), block_owner.astype(jnp.int32)))
    expert_new = adam_step(grad_expert, expert_param, expert_first, expert_second)
    return (latent_new[0], latent_new[1], latent_new[2], expert_new[0], expert_new[1], expert_new[2])
```

```python
import jax
import jax.numpy as jnp
from jax import lax
from jax.experimental import pallas as pl
from jax.experimental.pallas import tpu as pltpu
from jax.sharding import Mesh, PartitionSpec as P

STEP = 20
FIRST_BETA = 0.9
SECOND_BETA = 0.95
LEARNING_RATE = 0.1
WEIGHT_DECAY = 0.5
EPSILON = 1e-08

NZ, NY, CAP, SHARD, D, FFE = 16, 4, 88, 112, 7168, 1024
PAD = 128
N_DP = NZ * NY
EXTRA = FFE // NY // PAD
PARTS = NZ + EXTRA


def adam_step(gradient, weights, moment_one, moment_two):
    first_new = FIRST_BETA * moment_one + (1.0 - FIRST_BETA) * gradient
    second_new = SECOND_BETA * moment_two + (1.0 - SECOND_BETA) * gradient * gradient
    mean_hat = first_new / (1.0 - FIRST_BETA**STEP)
    scale_hat = second_new / (1.0 - SECOND_BETA**STEP)
    update = mean_hat / (jnp.sqrt(scale_hat) + EPSILON) + WEIGHT_DECAY * weights
    return (weights - LEARNING_RATE * update, first_new, second_new)


def pack_kernel(holder_ref, place_ref, x_ref, h_ref, out_ref):
    count, offset = place_ref[0], place_ref[1]
    row = lax.broadcasted_iota(jnp.int32, (CAP, CAP), 0)
    slot = lax.broadcasted_iota(jnp.int32, (CAP, CAP), 1)
    select = ((slot < count) & (row == slot + offset)).astype(jnp.float32).astype(jnp.bfloat16)
    source = lax.broadcasted_iota(jnp.int32, (2 * PAD, PAD), 0)
    lane = lax.broadcasted_iota(jnp.int32, (2 * PAD, PAD), 1)
    y = pl.program_id(0)
    for z in range(NZ):
        first = holder_ref[z * NY + y] * SHARD
        base = jnp.minimum(first // PAD, D // PAD - 2) * PAD
        window = x_ref[:, pl.ds(pl.multiple_of(base, PAD), 2 * PAD)]
        pick = ((source == lane + (first - base)) & (lane < SHARD)).astype(jnp.float32).astype(jnp.bfloat16)
        block = jnp.dot(window, pick, preferred_element_type=jnp.float32).astype(jnp.bfloat16)
        out_ref[0, z] = jnp.dot(select, block, preferred_element_type=jnp.float32).astype(jnp.bfloat16)
    for part in range(EXTRA):
        columns = pl.ds(pl.multiple_of((y * EXTRA + part) * PAD, PAD), PAD)
        out_ref[0, NZ + part] = jnp.dot(
            select, h_ref[:, columns], preferred_element_type=jnp.float32
        ).astype(jnp.bfloat16)


def pack(holder, place, rows, hidden):
    return pl.pallas_call(
        pack_kernel,
        out_shape=jax.ShapeDtypeStruct((NY, PARTS, CAP, PAD), jnp.bfloat16),
        grid_spec=pltpu.PrefetchScalarGridSpec(
            num_scalar_prefetch=2,
            grid=(NY,),
            in_specs=[
                pl.BlockSpec((CAP, D), lambda i, *_: (0, 0)),
                pl.BlockSpec((CAP, FFE), lambda i, *_: (0, 0)),
            ],
            out_specs=pl.BlockSpec((1, PARTS, CAP, PAD), lambda i, *_: (i, 0, 0, 0)),
        ),
        cost_estimate=pl.CostEstimate(
            flops=2 * N_DP * CAP * PAD * 400, bytes_accessed=3_000_000, transcendentals=0
        ),
        name="pack",
    )(holder, place, rows, hidden)


def on_device(
    attn_input,
    latent_grad,
    latent_param,
    latent_first,
    latent_second,
    expert_input,
    hidden_grad,
    counts,
    block_owner,
    expert_param,
    expert_first,
    expert_second,
):
    z, y = lax.axis_index("z"), lax.axis_index("y")
    expert = lax.axis_index("expert")
    position = z * NY + y
    own_counts = lax.dynamic_slice_in_dim(counts, expert, 1, 1)[:, 0]
    count = lax.dynamic_index_in_dim(own_counts, position, 0, keepdims=False)
    offset = jnp.where(y % 2 == 1, CAP - count, 0)
    blocks = jnp.arange(N_DP, dtype=jnp.int32)
    holder = jnp.sum(jnp.where(block_owner[0][:, None] == blocks[None, :], blocks[:, None], 0), axis=0)
    packed = pack(holder, jnp.stack([count, offset]), expert_input[0], hidden_grad[0])

    crossed = lax.all_to_all(packed, "y", split_axis=0, concat_axis=0, tiled=True)
    merged = crossed[0::2] + crossed[1::2]
    hidden_part = merged[:, NZ:].transpose(0, 2, 1, 3).reshape(2 * CAP, EXTRA * PAD)
    hidden = lax.all_gather(hidden_part, "z", axis=0, tiled=True)
    rows = merged[:, :NZ].transpose(1, 0, 2, 3)
    arrived = lax.all_to_all(rows, "z", split_axis=0, concat_axis=0, tiled=True)
    arrived = arrived.reshape(NZ * 2 * CAP, PAD)
    group = lax.all_gather(arrived, "y", axis=0, tiled=False)
    quarter = jnp.stack(
        [
            lax.dot_general(
                group[i], hidden, (((0,), (0,)), ((), ())), preferred_element_type=jnp.float32
            )[:SHARD]
            for i in range(NY)
        ]
    )
    grad_expert = lax.all_to_all(quarter, "y", split_axis=0, concat_axis=0, tiled=True)
    grad_expert = grad_expert.transpose(1, 0, 2).reshape(1, SHARD, FFE)
    expert_new = adam_step(grad_expert, expert_param, expert_first, expert_second)

    feat = attn_input.shape[1]
    shard = feat // N_DP
    wide = 16
    source = lax.broadcasted_iota(jnp.int32, (feat, N_DP * wide), 0)
    target = lax.broadcasted_iota(jnp.int32, (feat, N_DP * wide), 1)
    spread = (source == (target // wide) * shard + target % wide) & (target % wide < shard)
    columns = jnp.dot(
        attn_input, spread.astype(jnp.bfloat16), preferred_element_type=jnp.bfloat16
    )
    partial = lax.dot_general(
        columns, latent_grad, (((0,), (0,)), ((), ())), preferred_element_type=jnp.float32
    )
    grad_latent = lax.psum_scatter(partial, ("z", "y"), scatter_dimension=0, tiled=True)
    latent_new = adam_step(grad_latent[None, :shard], latent_param, latent_first, latent_second)
    return (*latent_new, *expert_new)


def solution(mesh):
    grid = Mesh(mesh.devices.reshape(NZ, NY, -1), ("z", "y", "expert"))
    dp = ("z", "y")
    sharded = P("expert", dp, None)
    return jax.shard_map(
        on_device,
        mesh=grid,
        in_specs=(
            P(dp, "expert"),
            P(dp, None),
            sharded,
            sharded,
            sharded,
            sharded,
            sharded,
            P(),
            P("expert", None),
            sharded,
            sharded,
            sharded,
        ),
        out_specs=(sharded,) * 6,
        check_vma=False,
    )
```

```python
import jax
import jax.numpy as jnp
from jax import lax
from jax.experimental import pallas as pl
from jax.experimental.pallas import tpu as pltpu
from jax.sharding import Mesh, PartitionSpec as P

STEP = 20
FIRST_BETA = 0.9
SECOND_BETA = 0.95
LEARNING_RATE = 0.1
WEIGHT_DECAY = 0.5
EPSILON = 1e-08

NZ, NY, CAP, SHARD, D, FFE = 16, 4, 88, 112, 7168, 1024
PAD = 128
N_DP = NZ * NY
EXTRA = FFE // NY // PAD
PARTS = NZ + EXTRA


def adam_step(gradient, weights, moment_one, moment_two):
    first_new = FIRST_BETA * moment_one + (1.0 - FIRST_BETA) * gradient
    second_new = SECOND_BETA * moment_two + (1.0 - SECOND_BETA) * gradient * gradient
    mean_hat = first_new / (1.0 - FIRST_BETA**STEP)
    scale_hat = second_new / (1.0 - SECOND_BETA**STEP)
    update = mean_hat / (jnp.sqrt(scale_hat) + EPSILON) + WEIGHT_DECAY * weights
    return (weights - LEARNING_RATE * update, first_new, second_new)


def pack_kernel(holder_ref, place_ref, x_ref, h_ref, out_ref):
    count, offset = place_ref[0], place_ref[1]
    row = lax.broadcasted_iota(jnp.int32, (CAP, CAP), 0)
    slot = lax.broadcasted_iota(jnp.int32, (CAP, CAP), 1)
    select = ((slot < count) & (row == slot + offset)).astype(jnp.float32).astype(jnp.bfloat16)
    source = lax.broadcasted_iota(jnp.int32, (2 * PAD, PAD), 0)
    lane = lax.broadcasted_iota(jnp.int32, (2 * PAD, PAD), 1)
    y = pl.program_id(0)
    for z in range(NZ):
        first = holder_ref[z * NY + y] * SHARD
        base = jnp.minimum(first // PAD, D // PAD - 2) * PAD
        window = x_ref[:, pl.ds(pl.multiple_of(base, PAD), 2 * PAD)]
        pick = ((source == lane + (first - base)) & (lane < SHARD)).astype(jnp.float32).astype(jnp.bfloat16)
        block = jnp.dot(window, pick, preferred_element_type=jnp.float32).astype(jnp.bfloat16)
        out_ref[0, z] = jnp.dot(select, block, preferred_element_type=jnp.float32).astype(jnp.bfloat16)
    for part in range(EXTRA):
        columns = pl.ds(pl.multiple_of((y * EXTRA + part) * PAD, PAD), PAD)
        out_ref[0, NZ + part] = jnp.dot(
            select, h_ref[:, columns], preferred_element_type=jnp.float32
        ).astype(jnp.bfloat16)


def pack(holder, place, rows, hidden):
    return pl.pallas_call(
        pack_kernel,
        out_shape=jax.ShapeDtypeStruct((NY, PARTS, CAP, PAD), jnp.bfloat16),
        grid_spec=pltpu.PrefetchScalarGridSpec(
            num_scalar_prefetch=2,
            grid=(NY,),
            in_specs=[
                pl.BlockSpec((CAP, D), lambda i, *_: (0, 0)),
                pl.BlockSpec((CAP, FFE), lambda i, *_: (0, 0)),
            ],
            out_specs=pl.BlockSpec((1, PARTS, CAP, PAD), lambda i, *_: (i, 0, 0, 0)),
        ),
        cost_estimate=pl.CostEstimate(
            flops=2 * N_DP * CAP * PAD * 400, bytes_accessed=3_000_000, transcendentals=0
        ),
        name="pack",
    )(holder, place, rows, hidden)


def merge_kernel(crossed_ref, rows_ref, hidden_ref):
    for pair in range(2):
        total = crossed_ref[2 * pair] + crossed_ref[2 * pair + 1]
        for z in range(NZ):
            rows_ref[z, pair] = total[z]
        for part in range(EXTRA):
            hidden_ref[pair * CAP : (pair + 1) * CAP, part * PAD : (part + 1) * PAD] = total[NZ + part]


def merge(crossed):
    whole = pl.BlockSpec(memory_space=pltpu.VMEM)
    return pl.pallas_call(
        merge_kernel,
        out_shape=(
            jax.ShapeDtypeStruct((NZ, 2, CAP, PAD), jnp.bfloat16),
            jax.ShapeDtypeStruct((2 * CAP, EXTRA * PAD), jnp.bfloat16),
        ),
        in_specs=[whole],
        out_specs=(whole, whole),
        cost_estimate=pl.CostEstimate(flops=1_000_000, bytes_accessed=2_500_000, transcendentals=0),
        name="merge",
    )(crossed)


def on_device(
    attn_input,
    latent_grad,
    latent_param,
    latent_first,
    latent_second,
    expert_input,
    hidden_grad,
    counts,
    block_owner,
    expert_param,
    expert_first,
    expert_second,
):
    z, y = lax.axis_index("z"), lax.axis_index("y")
    expert = lax.axis_index("expert")
    position = z * NY + y
    own_counts = lax.dynamic_slice_in_dim(counts, expert, 1, 1)[:, 0]
    count = lax.dynamic_index_in_dim(own_counts, position, 0, keepdims=False)
    offset = jnp.where(y % 2 == 1, CAP - count, 0)
    blocks = jnp.arange(N_DP, dtype=jnp.int32)
    holder = jnp.sum(jnp.where(block_owner[0][:, None] == blocks[None, :], blocks[:, None], 0), axis=0)
    packed = pack(holder, jnp.stack([count, offset]), expert_input[0], hidden_grad[0])

    crossed = lax.all_to_all(packed, "y", split_axis=0, concat_axis=0, tiled=True)
    rows, hidden_part = merge(crossed)
    hidden = lax.all_gather(hidden_part, "z", axis=0, tiled=True)
    arrived = lax.all_to_all(rows, "z", split_axis=0, concat_axis=0, tiled=True)
    arrived = arrived.reshape(NZ * 2 * CAP, PAD)
    arrived, hidden = lax.optimization_barrier((arrived, hidden))
    group = lax.all_gather(arrived, "y", axis=0, tiled=False)
    quarter = jnp.stack(
        [
            lax.dot_general(
                group[i], hidden, (((0,), (0,)), ((), ())), preferred_element_type=jnp.float32
            )[:SHARD]
            for i in range(NY)
        ]
    )
    grad_expert = lax.all_to_all(quarter, "y", split_axis=0, concat_axis=0, tiled=True)
    grad_expert = grad_expert.transpose(1, 0, 2).reshape(1, SHARD, FFE)
    expert_new = adam_step(grad_expert, expert_param, expert_first, expert_second)

    feat = attn_input.shape[1]
    shard = feat // N_DP
    wide = 16
    source = lax.broadcasted_iota(jnp.int32, (feat, N_DP * wide), 0)
    target = lax.broadcasted_iota(jnp.int32, (feat, N_DP * wide), 1)
    owner = (target // wide % NZ) * NY + target // wide // NZ
    spread = (source == owner * shard + target % wide) & (target % wide < shard)
    columns = jnp.dot(
        attn_input, spread.astype(jnp.bfloat16), preferred_element_type=jnp.bfloat16
    )
    partial = lax.dot_general(
        columns, latent_grad, (((0,), (0,)), ((), ())), preferred_element_type=jnp.float32
    )
    partial, _ = lax.optimization_barrier((partial, arrived))
    parts = lax.all_to_all(
        partial.reshape(NY, NZ * wide, -1), "y", split_axis=0, concat_axis=0, tiled=True
    )
    parts = lax.all_to_all(
        jnp.sum(parts, axis=0).reshape(NZ, wide, -1), "z", split_axis=0, concat_axis=0, tiled=True
    )
    grad_latent = jnp.sum(parts, axis=0)
    latent_new = adam_step(grad_latent[None, :shard], latent_param, latent_first, latent_second)
    return (*latent_new, *expert_new)


def solution(mesh):
    grid = Mesh(mesh.devices.reshape(NZ, NY, -1), ("z", "y", "expert"))
    dp = ("z", "y")
    sharded = P("expert", dp, None)
    return jax.shard_map(
        on_device,
        mesh=grid,
        in_specs=(
            P(dp, "expert"),
            P(dp, None),
            sharded,
            sharded,
            sharded,
            sharded,
            sharded,
            P(),
            P("expert", None),
            sharded,
            sharded,
            sharded,
        ),
        out_specs=(sharded,) * 6,
        check_vma=False,
    )
```

```python
import jax
import jax.numpy as jnp
from jax import lax
from jax.experimental import pallas as pl
from jax.experimental.pallas import tpu as pltpu
from jax.sharding import Mesh, PartitionSpec as P

STEP = 20
FIRST_BETA = 0.9
SECOND_BETA = 0.95
LEARNING_RATE = 0.1
WEIGHT_DECAY = 0.5
EPSILON = 1e-08

NZ, NY, CAP, SHARD, D, FFE = 16, 4, 88, 112, 7168, 1024
PAD = 128
N_DP = NZ * NY
EXTRA = FFE // NY // PAD
PARTS = NZ + EXTRA


def adam_step(gradient, weights, moment_one, moment_two):
    first_new = FIRST_BETA * moment_one + (1.0 - FIRST_BETA) * gradient
    second_new = SECOND_BETA * moment_two + (1.0 - SECOND_BETA) * gradient * gradient
    mean_hat = first_new / (1.0 - FIRST_BETA**STEP)
    scale_hat = second_new / (1.0 - SECOND_BETA**STEP)
    update = mean_hat / (jnp.sqrt(scale_hat) + EPSILON) + WEIGHT_DECAY * weights
    return (weights - LEARNING_RATE * update, first_new, second_new)


def pack_kernel(holder_ref, place_ref, x_ref, h_ref, out_ref):
    count, offset = place_ref[0], place_ref[1]
    row = lax.broadcasted_iota(jnp.int32, (CAP, CAP), 0)
    slot = lax.broadcasted_iota(jnp.int32, (CAP, CAP), 1)
    select = ((slot < count) & (row == slot + offset)).astype(jnp.float32).astype(jnp.bfloat16)
    source = lax.broadcasted_iota(jnp.int32, (2 * PAD, PAD), 0)
    lane = lax.broadcasted_iota(jnp.int32, (2 * PAD, PAD), 1)
    y = pl.program_id(0)
    for z in range(NZ):
        first = holder_ref[z * NY + y] * SHARD
        base = jnp.minimum(first // PAD, D // PAD - 2) * PAD
        window = x_ref[:, pl.ds(pl.multiple_of(base, PAD), 2 * PAD)]
        pick = ((source == lane + (first - base)) & (lane < SHARD)).astype(jnp.float32).astype(jnp.bfloat16)
        block = jnp.dot(window, pick, preferred_element_type=jnp.float32).astype(jnp.bfloat16)
        out_ref[0, z] = jnp.dot(select, block, preferred_element_type=jnp.float32).astype(jnp.bfloat16)
    for part in range(EXTRA):
        columns = pl.ds(pl.multiple_of((y * EXTRA + part) * PAD, PAD), PAD)
        out_ref[0, NZ + part] = jnp.dot(
            select, h_ref[:, columns], preferred_element_type=jnp.float32
        ).astype(jnp.bfloat16)


def pack(holder, place, rows, hidden):
    return pl.pallas_call(
        pack_kernel,
        out_shape=jax.ShapeDtypeStruct((NY, PARTS, CAP, PAD), jnp.bfloat16),
        grid_spec=pltpu.PrefetchScalarGridSpec(
            num_scalar_prefetch=2,
            grid=(NY,),
            in_specs=[
                pl.BlockSpec((CAP, D), lambda i, *_: (0, 0)),
                pl.BlockSpec((CAP, FFE), lambda i, *_: (0, 0)),
            ],
            out_specs=pl.BlockSpec((1, PARTS, CAP, PAD), lambda i, *_: (i, 0, 0, 0)),
        ),
        cost_estimate=pl.CostEstimate(
            flops=2 * N_DP * CAP * PAD * 400, bytes_accessed=3_000_000, transcendentals=0
        ),
        name="pack",
    )(holder, place, rows, hidden)


def merge_kernel(crossed_ref, rows_ref, hidden_ref):
    for pair in range(2):
        total = crossed_ref[2 * pair] + crossed_ref[2 * pair + 1]
        for z in range(NZ):
            rows_ref[z, pair] = total[z]
        for part in range(EXTRA):
            hidden_ref[pair * CAP : (pair + 1) * CAP, part * PAD : (part + 1) * PAD] = total[NZ + part]


def merge(crossed):
    whole = pl.BlockSpec(memory_space=pltpu.VMEM)
    return pl.pallas_call(
        merge_kernel,
        out_shape=(
            jax.ShapeDtypeStruct((NZ, 2, CAP, PAD), jnp.bfloat16),
            jax.ShapeDtypeStruct((2 * CAP, EXTRA * PAD), jnp.bfloat16),
        ),
        in_specs=[whole],
        out_specs=(whole, whole),
        cost_estimate=pl.CostEstimate(flops=1_000_000, bytes_accessed=2_500_000, transcendentals=0),
        name="merge",
    )(crossed)


MESH = pl.DeviceIdType.MESH


def exchange_kernel(
    rows_ref, hid_ref, part_ref, group_ref, hidden_ref, total_ref, crossed, summed, landed,
    local, ring_send, ring_recv, x_send, x_recv, f_send, f_recv, y_send, y_recv, l_send, l_recv,
):
    z, y = lax.axis_index("z"), lax.axis_index("y")

    def at_z(d):
        return lax.rem(z + d + NZ, NZ)

    def at_y(d):
        return lax.rem(y + d, NY)

    def remote(src, dst, send, recv, **where):
        return pltpu.make_async_remote_copy(
            src_ref=src, dst_ref=dst, send_sem=send, recv_sem=recv, device_id=where, device_id_type=MESH
        )

    def ring(way, s):
        block = hidden_ref.at[at_z(-s if way == 0 else s)]
        return remote(
            block, block, ring_send.at[way, s], ring_recv.at[way, s], z=at_z(1 if way == 0 else -1)
        )

    def push(d):
        return remote(
            rows_ref.at[at_z(d)], group_ref.at[y, z], x_send.at[d], x_recv.at[d], z=at_z(d)
        )

    def forward(d, e):
        block = group_ref.at[y, at_z(-d)]
        return remote(block, block, f_send.at[d, e], f_recv.at[d, e], y=at_y(e))

    def latent_y(d):
        return remote(part_ref.at[at_y(d)], crossed.at[d - 1], y_send.at[d], y_recv.at[d], y=at_y(d))

    def latent_z(d):
        return remote(summed.at[at_z(d)], landed.at[d], l_send.at[d], l_recv.at[d], z=at_z(d))

    def each(first, last, step):
        lax.fori_loop(first, last, lambda i, _: (step(i), 0)[1], 0)

    barrier = pltpu.get_barrier_semaphore()
    each(1, NZ, lambda d: pl.semaphore_signal(barrier, inc=1, device_id={"z": at_z(d)}, device_id_type=MESH))
    each(1, NY, lambda d: pl.semaphore_signal(barrier, inc=1, device_id={"y": at_y(d)}, device_id_type=MESH))
    pl.semaphore_wait(barrier, NZ + NY - 2)

    keep = pltpu.make_async_copy(hid_ref, hidden_ref.at[z], local.at[0])
    own = pltpu.make_async_copy(rows_ref.at[z], group_ref.at[y, z], local.at[1])
    keep.start()
    own.start()
    keep.wait()
    ring(0, 0).start()
    ring(1, 0).start()
    each(1, NZ, lambda d: push(d).start())
    each(1, NY, lambda d: latent_y(d).start())
    own.wait()
    each(1, NY, lambda e: forward(0, e).start())

    def step(s):
        ring(0, s - 1).wait_recv()
        ring(0, s).start()
        ring(1, s - 1).wait_recv()
        ring(1, s).start()
        push(s).wait_recv()
        each(1, NY, lambda e: forward(s, e).start())
        push(NZ - s).wait_recv()
        each(1, NY, lambda e: forward(NZ - s, e).start())

    half = NZ // 2
    each(1, 4, step)
    each(1, NY, lambda d: latent_y(d).wait_recv())
    summed[...] = (part_ref[y] + crossed[0] + crossed[1] + crossed[2]).reshape(summed.shape)
    each(4, 6, step)
    each(1, NZ, lambda d: latent_z(d).start())
    each(6, half - 1, step)
    last = half - 1
    ring(0, last - 1).wait_recv()
    ring(0, last).start()
    ring(1, last - 1).wait_recv()
    for d in (last, NZ - last, half):
        push(d).wait_recv()
        each(1, NY, lambda e: forward(d, e).start())
    ring(0, last).wait_recv()

    each(1, NZ, lambda d: latent_z(d).wait_recv())
    total = summed[z]
    for d in range(1, NZ):
        total = total + landed[d]
    total_ref[...] = total

    def drain(d):
        each(1, NY, lambda e: forward(d, e).wait())

    each(0, NZ, drain)
    each(0, last, lambda s: ring(1, s).wait_send())
    each(0, half, lambda s: ring(0, s).wait_send())
    each(1, NZ, lambda d: push(d).wait_send())
    each(1, NY, lambda d: latent_y(d).wait_send())
    each(1, NZ, lambda d: latent_z(d).wait_send())


def exchange(rows, hidden_part, partial):
    whole = pl.BlockSpec(memory_space=pltpu.VMEM)
    wide, lat = partial.shape[1] // NZ, partial.shape[2]
    dma = pltpu.SemaphoreType.DMA
    return pl.pallas_call(
        exchange_kernel,
        out_shape=(
            jax.ShapeDtypeStruct((NY, NZ, 2 * CAP, PAD), jnp.bfloat16),
            jax.ShapeDtypeStruct((NZ, 2 * CAP, EXTRA * PAD), jnp.bfloat16),
            jax.ShapeDtypeStruct((wide, lat), jnp.float32),
        ),
        in_specs=[whole] * 3,
        out_specs=(whole,) * 3,
        scratch_shapes=[
            pltpu.VMEM((NY - 1, NZ * wide, lat), jnp.float32),
            pltpu.VMEM((NZ, wide, lat), jnp.float32),
            pltpu.VMEM((NZ, wide, lat), jnp.float32),
            dma((2,)),
            dma((2, NZ // 2)),
            dma((2, NZ // 2)),
            dma((NZ,)),
            dma((NZ,)),
            dma((NZ, NY)),
            dma((NZ, NY)),
            dma((NY,)),
            dma((NY,)),
            dma((NZ,)),
            dma((NZ,)),
        ],
        compiler_params=pltpu.CompilerParams(collective_id=0, has_side_effects=True),
        name="exchange",
    )(rows, hidden_part, partial)


def on_device(
    attn_input,
    latent_grad,
    latent_param,
    latent_first,
    latent_second,
    expert_input,
    hidden_grad,
    counts,
    block_owner,
    expert_param,
    expert_first,
    expert_second,
):
    z, y = lax.axis_index("z"), lax.axis_index("y")
    expert = lax.axis_index("expert")
    position = z * NY + y
    own_counts = lax.dynamic_slice_in_dim(counts, expert, 1, 1)[:, 0]
    count = lax.dynamic_index_in_dim(own_counts, position, 0, keepdims=False)
    offset = jnp.where(y % 2 == 1, CAP - count, 0)
    blocks = jnp.arange(N_DP, dtype=jnp.int32)
    holder = jnp.sum(jnp.where(block_owner[0][:, None] == blocks[None, :], blocks[:, None], 0), axis=0)
    packed = pack(holder, jnp.stack([count, offset]), expert_input[0], hidden_grad[0])

    crossed = lax.all_to_all(packed, "y", split_axis=0, concat_axis=0, tiled=True)
    rows, hidden_part = merge(crossed)
    feat = attn_input.shape[1]
    shard = feat // N_DP
    wide = 16
    source = lax.broadcasted_iota(jnp.int32, (feat, N_DP * wide), 0)
    target = lax.broadcasted_iota(jnp.int32, (feat, N_DP * wide), 1)
    owner = (target // wide % NZ) * NY + target // wide // NZ
    spread = (source == owner * shard + target % wide) & (target % wide < shard)
    columns = jnp.dot(
        attn_input, spread.astype(jnp.bfloat16), preferred_element_type=jnp.bfloat16
    )
    partial = lax.dot_general(
        columns, latent_grad, (((0,), (0,)), ((), ())), preferred_element_type=jnp.float32
    )
    group, hidden, grad_latent = exchange(
        rows.reshape(NZ, 2 * CAP, PAD), hidden_part, partial.reshape(NY, NZ * wide, -1)
    )
    group = group.reshape(NY, NZ * 2 * CAP, PAD)
    hidden = hidden.reshape(NZ * 2 * CAP, EXTRA * PAD)
    quarter = jnp.stack(
        [
            lax.dot_general(
                group[i], hidden, (((0,), (0,)), ((), ())), preferred_element_type=jnp.float32
            )[:SHARD]
            for i in range(NY)
        ]
    )
    grad_expert = lax.all_to_all(quarter, "y", split_axis=0, concat_axis=0, tiled=True)
    grad_expert = grad_expert.transpose(1, 0, 2).reshape(1, SHARD, FFE)
    expert_new = adam_step(grad_expert, expert_param, expert_first, expert_second)

    latent_new = adam_step(grad_latent[None, :shard], latent_param, latent_first, latent_second)
    return (*latent_new, *expert_new)


def solution(mesh):
    grid = Mesh(mesh.devices.reshape(NZ, NY, -1), ("z", "y", "expert"))
    dp = ("z", "y")
    sharded = P("expert", dp, None)
    return jax.shard_map(
        on_device,
        mesh=grid,
        in_specs=(
            P(dp, "expert"),
            P(dp, None),
            sharded,
            sharded,
            sharded,
            sharded,
            sharded,
            P(),
            P("expert", None),
            sharded,
            sharded,
            sharded,
        ),
        out_specs=(sharded,) * 6,
        check_vma=False,
    )
```

```python
import jax
import jax.numpy as jnp
from jax import lax
from jax.experimental import pallas as pl
from jax.experimental.pallas import tpu as pltpu
from jax.sharding import Mesh, PartitionSpec as P

STEP = 20
FIRST_BETA = 0.9
SECOND_BETA = 0.95
LEARNING_RATE = 0.1
WEIGHT_DECAY = 0.5
EPSILON = 1e-08

NZ, NY, CAP, SHARD, D, FFE = 16, 4, 88, 112, 7168, 1024
PAD = 128
N_DP = NZ * NY
EXTRA = FFE // NY // PAD
PARTS = NZ + EXTRA
CUT = 96


def adam_step(gradient, weights, moment_one, moment_two):
    first_new = FIRST_BETA * moment_one + (1.0 - FIRST_BETA) * gradient
    second_new = SECOND_BETA * moment_two + (1.0 - SECOND_BETA) * gradient * gradient
    mean_hat = first_new / (1.0 - FIRST_BETA**STEP)
    scale_hat = second_new / (1.0 - SECOND_BETA**STEP)
    update = mean_hat / (jnp.sqrt(scale_hat) + EPSILON) + WEIGHT_DECAY * weights
    return (weights - LEARNING_RATE * update, first_new, second_new)


def pack_kernel(holder_ref, place_ref, x_ref, h_ref, out_ref):
    count, offset = place_ref[0], place_ref[1]
    row = lax.broadcasted_iota(jnp.int32, (CAP, CAP), 0)
    slot = lax.broadcasted_iota(jnp.int32, (CAP, CAP), 1)
    select = ((slot < count) & (row == slot + offset)).astype(jnp.float32).astype(jnp.bfloat16)
    source = lax.broadcasted_iota(jnp.int32, (2 * PAD, PAD), 0)
    lane = lax.broadcasted_iota(jnp.int32, (2 * PAD, PAD), 1)
    y = pl.program_id(0)
    for z in range(NZ):
        first = holder_ref[z * NY + y] * SHARD
        base = jnp.minimum(first // PAD, D // PAD - 2) * PAD
        window = x_ref[:, pl.ds(pl.multiple_of(base, PAD), 2 * PAD)]
        pick = ((source == lane + (first - base)) & (lane < SHARD)).astype(jnp.float32).astype(jnp.bfloat16)
        block = jnp.dot(window, pick, preferred_element_type=jnp.float32).astype(jnp.bfloat16)
        out_ref[0, z] = jnp.dot(select, block, preferred_element_type=jnp.float32).astype(jnp.bfloat16)
    for part in range(EXTRA):
        columns = pl.ds(pl.multiple_of((y * EXTRA + part) * PAD, PAD), PAD)
        out_ref[0, NZ + part] = jnp.dot(
            select, h_ref[:, columns], preferred_element_type=jnp.float32
        ).astype(jnp.bfloat16)


def pack(holder, place, rows, hidden):
    return pl.pallas_call(
        pack_kernel,
        out_shape=jax.ShapeDtypeStruct((NY, PARTS, CAP, PAD), jnp.bfloat16),
        grid_spec=pltpu.PrefetchScalarGridSpec(
            num_scalar_prefetch=2,
            grid=(NY,),
            in_specs=[
                pl.BlockSpec((CAP, D), lambda i, *_: (0, 0)),
                pl.BlockSpec((CAP, FFE), lambda i, *_: (0, 0)),
            ],
            out_specs=pl.BlockSpec((1, PARTS, CAP, PAD), lambda i, *_: (i, 0, 0, 0)),
        ),
        cost_estimate=pl.CostEstimate(
            flops=2 * N_DP * CAP * PAD * 400, bytes_accessed=3_000_000, transcendentals=0
        ),
        name="pack",
    )(holder, place, rows, hidden)


def merge_kernel(crossed_ref, rows_ref, hidden_ref):
    for pair in range(2):
        total = crossed_ref[2 * pair] + crossed_ref[2 * pair + 1]
        for z in range(NZ):
            rows_ref[z, pair] = total[z]
        for part in range(EXTRA):
            hidden_ref[pair * CAP : (pair + 1) * CAP, part * PAD : (part + 1) * PAD] = total[NZ + part]


def merge(crossed):
    whole = pl.BlockSpec(memory_space=pltpu.VMEM)
    return pl.pallas_call(
        merge_kernel,
        out_shape=(
            jax.ShapeDtypeStruct((NZ, 2, CAP, PAD), jnp.bfloat16),
            jax.ShapeDtypeStruct((2 * CAP, EXTRA * PAD), jnp.bfloat16),
        ),
        in_specs=[whole],
        out_specs=(whole, whole),
        cost_estimate=pl.CostEstimate(flops=1_000_000, bytes_accessed=2_500_000, transcendentals=0),
        name="merge",
    )(crossed)


MESH = pl.DeviceIdType.MESH


def exchange_kernel(
    rows_ref, hid_ref, part_ref, group_ref, hidden_ref, total_ref, crossed, middle, summed, carry, landed,
    local, ring_send, ring_recv, x_send, x_recv, f_send, f_recv, r_send, r_recv, y_send, y_recv,
    m_send, m_recv, l_send, l_recv,
):
    z, y = lax.axis_index("z"), lax.axis_index("y")

    def at_z(d):
        return lax.rem(z + d + NZ, NZ)

    def at_y(d):
        return lax.rem(y + d, NY)

    def remote(src, dst, send, recv, **where):
        return pltpu.make_async_remote_copy(
            src_ref=src, dst_ref=dst, send_sem=send, recv_sem=recv, device_id=where, device_id_type=MESH
        )

    def ring(way, s):
        block = hidden_ref.at[at_z(-s if way == 0 else s)]
        return remote(
            block, block, ring_send.at[way, s], ring_recv.at[way, s], z=at_z(1 if way == 0 else -1)
        )

    def push(d):
        return remote(
            rows_ref.at[at_z(d)], group_ref.at[y, z], x_send.at[d], x_recv.at[d], z=at_z(d)
        )

    def forward(d, e):
        block = group_ref.at[y, at_z(-d)]
        return remote(block, block, f_send.at[d, e], f_recv.at[d, e], y=at_y(e))

    def relay(d, way):
        from_y, cut = (at_y(3), pl.ds(0, CUT)) if way == 0 else (at_y(1), pl.ds(CUT, 2 * CAP - CUT))
        block = group_ref.at[from_y, at_z(-d), cut]
        return remote(block, block, r_send.at[way, d], r_recv.at[way, d], y=at_y(1 if way == 0 else 3))

    def latent_y(d):
        return remote(part_ref.at[at_y(d)], crossed.at[d - 1], y_send.at[d], y_recv.at[d], y=at_y(d))

    mid = part_ref.shape[1] // 2

    def latent_out(way):
        return remote(
            part_ref.at[at_y(2), pl.ds(way * mid, mid)], middle.at[way],
            m_send.at[0, way], m_recv.at[0, way], y=at_y(1 if way == 0 else 3),
        )

    def latent_on(way):
        return remote(
            middle.at[way], crossed.at[1, pl.ds(way * mid, mid)],
            m_send.at[1, way], m_recv.at[1, way], y=at_y(1 if way == 0 else 3),
        )

    def latent_z(way, s):
        return remote(
            carry.at[way, s], landed.at[way, s], l_send.at[way, s], l_recv.at[way, s],
            z=at_z(1 if way == 0 else -1),
        )

    def term(way, s):
        return summed[at_z(NZ // 2 - s if way == 0 else s - NZ // 2 + 1)]

    def each(first, last, step):
        lax.fori_loop(first, last, lambda i, _: (step(i), 0)[1], 0)

    barrier = pltpu.get_barrier_semaphore()
    each(1, NZ, lambda d: pl.semaphore_signal(barrier, inc=1, device_id={"z": at_z(d)}, device_id_type=MESH))
    each(1, NY, lambda d: pl.semaphore_signal(barrier, inc=1, device_id={"y": at_y(d)}, device_id_type=MESH))
    pl.semaphore_wait(barrier, NZ + NY - 2)

    keep = pltpu.make_async_copy(hid_ref, hidden_ref.at[z], local.at[0])
    own = pltpu.make_async_copy(rows_ref.at[z], group_ref.at[y, z], local.at[1])
    keep.start()
    own.start()
    keep.wait()
    ring(0, 0).start()
    ring(1, 0).start()
    for way in range(2):
        latent_out(way).start()
    latent_y(1).start()
    latent_y(3).start()
    each(1, NZ, lambda d: push(d).start())
    own.wait()

    def spread(d):
        forward(d, 1).start()
        forward(d, 3).start()

    def relays(d):
        forward(d, 1).wait_recv()
        relay(d, 0).start()
        forward(d, 3).wait_recv()
        relay(d, 1).start()

    spread(0)
    half = NZ // 2
    last = half - 1

    def step(s):
        ring(0, s - 1).wait_recv()
        ring(0, s).start()
        ring(1, s - 1).wait_recv()
        ring(1, s).start()
        push(s).wait_recv()
        spread(s)
        push(NZ - s).wait_recv()
        spread(NZ - s)

    def both(s):
        step(s)
        relays(s - 1)
        relays(NZ - s + 1)

    def add_on(way, s):
        latent_z(way, s - 1).wait_recv()
        carry[way, s] = landed[way, s - 1] + term(way, s)
        latent_z(way, s).start()

    step(1)
    for way in range(2):
        latent_out(way).wait_recv()
        latent_on(way).start()
    relays(0)
    each(2, 4, both)
    latent_y(1).wait_recv()
    latent_y(3).wait_recv()
    for way in range(2):
        latent_on(way).wait_recv()
    summed[...] = (part_ref[y] + crossed[0] + crossed[1] + crossed[2]).reshape(summed.shape)
    for way in range(2):
        carry[way, 0] = term(way, 0)
    both(4)
    for way in range(2):
        latent_z(way, 0).start()

    def all_three(s):
        both(s)
        add_on(0, s - 4)
        add_on(1, s - 4)

    each(5, last, all_three)
    ring(0, last - 1).wait_recv()
    ring(0, last).start()
    ring(1, last - 1).wait_recv()
    for d in (last, NZ - last, half):
        push(d).wait_recv()
        spread(d)
    relays(last - 1)
    relays(NZ - last + 1)
    add_on(0, 3)
    add_on(1, 3)
    for d in (last, NZ - last, half):
        relays(d)

    def add_both(s):
        add_on(0, s)
        add_on(1, s)

    each(4, last, add_both)
    add_on(0, last)
    latent_z(1, last - 1).wait_recv()
    latent_z(0, last).wait_recv()
    total_ref[...] = summed[z] + landed[0, last] + landed[1, last - 1]
    ring(0, last).wait_recv()

    def drain(d):
        forward(d, 1).wait_send()
        forward(d, 3).wait_send()
        relay(d, 0).wait()
        relay(d, 1).wait()

    each(0, NZ, drain)

    def drain_rings(s):
        ring(0, s).wait_send()
        ring(1, s).wait_send()
        latent_z(0, s).wait_send()
        latent_z(1, s).wait_send()

    each(0, last, drain_rings)
    ring(0, last).wait_send()
    latent_z(0, last).wait_send()
    each(1, NZ, lambda d: push(d).wait_send())
    for way in range(2):
        latent_out(way).wait_send()
        latent_on(way).wait_send()
    latent_y(1).wait_send()
    latent_y(3).wait_send()


def exchange(rows, hidden_part, partial):
    whole = pl.BlockSpec(memory_space=pltpu.VMEM)
    wide, lat = partial.shape[1] // NZ, partial.shape[2]
    dma = pltpu.SemaphoreType.DMA
    return pl.pallas_call(
        exchange_kernel,
        out_shape=(
            jax.ShapeDtypeStruct((NY, NZ, 2 * CAP, PAD), jnp.bfloat16),
            jax.ShapeDtypeStruct((NZ, 2 * CAP, EXTRA * PAD), jnp.bfloat16),
            jax.ShapeDtypeStruct((wide, lat), jnp.float32),
        ),
        in_specs=[whole] * 3,
        out_specs=(whole,) * 3,
        scratch_shapes=[
            pltpu.VMEM((NY - 1, NZ * wide, lat), jnp.float32),
            pltpu.VMEM((2, NZ * wide // 2, lat), jnp.float32),
            pltpu.VMEM((NZ, wide, lat), jnp.float32),
            pltpu.VMEM((2, NZ // 2, wide, lat), jnp.float32),
            pltpu.VMEM((2, NZ // 2, wide, lat), jnp.float32),
            dma((2,)),
            dma((2, NZ // 2)),
            dma((2, NZ // 2)),
            dma((NZ,)),
            dma((NZ,)),
            dma((NZ, NY)),
            dma((NZ, NY)),
            dma((2, NZ)),
            dma((2, NZ)),
            dma((NY,)),
            dma((NY,)),
            dma((2, 2)),
            dma((2, 2)),
            dma((2, NZ // 2)),
            dma((2, NZ // 2)),
        ],
        compiler_params=pltpu.CompilerParams(collective_id=0, has_side_effects=True),
        name="exchange",
    )(rows, hidden_part, partial)


def on_device(
    attn_input,
    latent_grad,
    latent_param,
    latent_first,
    latent_second,
    expert_input,
    hidden_grad,
    counts,
    block_owner,
    expert_param,
    expert_first,
    expert_second,
):
    z, y = lax.axis_index("z"), lax.axis_index("y")
    expert = lax.axis_index("expert")
    position = z * NY + y
    own_counts = lax.dynamic_slice_in_dim(counts, expert, 1, 1)[:, 0]
    count = lax.dynamic_index_in_dim(own_counts, position, 0, keepdims=False)
    offset = jnp.where(y % 2 == 1, CAP - count, 0)
    blocks = jnp.arange(N_DP, dtype=jnp.int32)
    holder = jnp.sum(jnp.where(block_owner[0][:, None] == blocks[None, :], blocks[:, None], 0), axis=0)
    packed = pack(holder, jnp.stack([count, offset]), expert_input[0], hidden_grad[0])

    crossed = lax.all_to_all(packed, "y", split_axis=0, concat_axis=0, tiled=True)
    rows, hidden_part = merge(crossed)
    feat = attn_input.shape[1]
    shard = feat // N_DP
    wide = 16
    source = lax.broadcasted_iota(jnp.int32, (feat, N_DP * wide), 0)
    target = lax.broadcasted_iota(jnp.int32, (feat, N_DP * wide), 1)
    owner = (target // wide % NZ) * NY + target // wide // NZ
    spread = (source == owner * shard + target % wide) & (target % wide < shard)
    columns = jnp.dot(
        attn_input, spread.astype(jnp.bfloat16), preferred_element_type=jnp.bfloat16
    )
    partial = lax.dot_general(
        columns, latent_grad, (((0,), (0,)), ((), ())), preferred_element_type=jnp.float32
    )
    group, hidden, grad_latent = exchange(
        rows.reshape(NZ, 2 * CAP, PAD), hidden_part, partial.reshape(NY, NZ * wide, -1)
    )
    group = group.reshape(NY, NZ * 2 * CAP, PAD)
    hidden = hidden.reshape(NZ * 2 * CAP, EXTRA * PAD)
    quarter = jnp.stack(
        [
            lax.dot_general(
                group[i], hidden, (((0,), (0,)), ((), ())), preferred_element_type=jnp.float32
            )[:SHARD]
            for i in range(NY)
        ]
    )
    grad_expert = lax.all_to_all(quarter, "y", split_axis=0, concat_axis=0, tiled=True)
    grad_expert = grad_expert.transpose(1, 0, 2).reshape(1, SHARD, FFE)
    expert_new = adam_step(grad_expert, expert_param, expert_first, expert_second)

    latent_new = adam_step(grad_latent[None, :shard], latent_param, latent_first, latent_second)
    return (*latent_new, *expert_new)


def solution(mesh):
    grid = Mesh(mesh.devices.reshape(NZ, NY, -1), ("z", "y", "expert"))
    dp = ("z", "y")
    sharded = P("expert", dp, None)
    return jax.shard_map(
        on_device,
        mesh=grid,
        in_specs=(
            P(dp, "expert"),
            P(dp, None),
            sharded,
            sharded,
            sharded,
            sharded,
            sharded,
            P(),
            P("expert", None),
            sharded,
            sharded,
            sharded,
        ),
        out_specs=(sharded,) * 6,
        check_vma=False,
    )
```

```python
import jax
import jax.numpy as jnp
from jax import lax
from jax.experimental import pallas as pl
from jax.experimental.pallas import tpu as pltpu
from jax.sharding import Mesh, PartitionSpec as P

STEP = 20
FIRST_BETA = 0.9
SECOND_BETA = 0.95
LEARNING_RATE = 0.1
WEIGHT_DECAY = 0.5
EPSILON = 1e-08

NZ, NY, CAP, SHARD, D, FFE = 16, 4, 88, 112, 7168, 1024
PAD = 128
N_DP = NZ * NY
EXTRA = FFE // NY // PAD
PARTS = NZ + EXTRA
CUT = 96


def adam_step(gradient, weights, moment_one, moment_two):
    first_new = FIRST_BETA * moment_one + (1.0 - FIRST_BETA) * gradient
    second_new = SECOND_BETA * moment_two + (1.0 - SECOND_BETA) * gradient * gradient
    mean_hat = first_new / (1.0 - FIRST_BETA**STEP)
    scale_hat = second_new / (1.0 - SECOND_BETA**STEP)
    update = mean_hat / (jnp.sqrt(scale_hat) + EPSILON) + WEIGHT_DECAY * weights
    return (weights - LEARNING_RATE * update, first_new, second_new)


def pack_kernel(holder_ref, place_ref, x_ref, h_ref, out_ref):
    count, offset = place_ref[0], place_ref[1]
    row = lax.broadcasted_iota(jnp.int32, (CAP, CAP), 0)
    slot = lax.broadcasted_iota(jnp.int32, (CAP, CAP), 1)
    select = ((slot < count) & (row == slot + offset)).astype(jnp.float32).astype(jnp.bfloat16)
    source = lax.broadcasted_iota(jnp.int32, (2 * PAD, PAD), 0)
    lane = lax.broadcasted_iota(jnp.int32, (2 * PAD, PAD), 1)
    y = pl.program_id(0)
    for z in range(NZ):
        first = holder_ref[z * NY + y] * SHARD
        base = jnp.minimum(first // PAD, D // PAD - 2) * PAD
        window = x_ref[:, pl.ds(pl.multiple_of(base, PAD), 2 * PAD)]
        pick = ((source == lane + (first - base)) & (lane < SHARD)).astype(jnp.float32).astype(jnp.bfloat16)
        block = jnp.dot(window, pick, preferred_element_type=jnp.float32).astype(jnp.bfloat16)
        out_ref[0, z] = jnp.dot(select, block, preferred_element_type=jnp.float32).astype(jnp.bfloat16)
    for part in range(EXTRA):
        columns = pl.ds(pl.multiple_of((y * EXTRA + part) * PAD, PAD), PAD)
        out_ref[0, NZ + part] = jnp.dot(
            select, h_ref[:, columns], preferred_element_type=jnp.float32
        ).astype(jnp.bfloat16)


def pack(holder, place, rows, hidden):
    return pl.pallas_call(
        pack_kernel,
        out_shape=jax.ShapeDtypeStruct((NY, PARTS, CAP, PAD), jnp.bfloat16),
        grid_spec=pltpu.PrefetchScalarGridSpec(
            num_scalar_prefetch=2,
            grid=(NY,),
            in_specs=[
                pl.BlockSpec((CAP, D), lambda i, *_: (0, 0)),
                pl.BlockSpec((CAP, FFE), lambda i, *_: (0, 0)),
            ],
            out_specs=pl.BlockSpec((1, PARTS, CAP, PAD), lambda i, *_: (i, 0, 0, 0)),
        ),
        cost_estimate=pl.CostEstimate(
            flops=2 * N_DP * CAP * PAD * 400, bytes_accessed=3_000_000, transcendentals=0
        ),
        name="pack",
    )(holder, place, rows, hidden)


def merge_kernel(crossed_ref, rows_ref, hidden_ref):
    for pair in range(2):
        total = crossed_ref[2 * pair] + crossed_ref[2 * pair + 1]
        for z in range(NZ):
            rows_ref[z, pair] = total[z]
        for part in range(EXTRA):
            hidden_ref[pair * CAP : (pair + 1) * CAP, part * PAD : (part + 1) * PAD] = total[NZ + part]


def merge(crossed):
    whole = pl.BlockSpec(memory_space=pltpu.VMEM)
    return pl.pallas_call(
        merge_kernel,
        out_shape=(
            jax.ShapeDtypeStruct((NZ, 2, CAP, PAD), jnp.bfloat16),
            jax.ShapeDtypeStruct((2 * CAP, EXTRA * PAD), jnp.bfloat16),
        ),
        in_specs=[whole],
        out_specs=(whole, whole),
        cost_estimate=pl.CostEstimate(flops=1_000_000, bytes_accessed=2_500_000, transcendentals=0),
        name="merge",
    )(crossed)


MESH = pl.DeviceIdType.MESH


def exchange_kernel(
    rows_ref, hid_ref, part_ref, group_ref, hidden_ref, total_ref, crossed, middle, summed, carry, landed,
    local, ring_send, ring_recv, x_send, x_recv, f_send, f_recv, r_send, r_recv, y_send, y_recv,
    m_send, m_recv, l_send, l_recv,
):
    z, y = lax.axis_index("z"), lax.axis_index("y")

    def at_z(d):
        return lax.rem(z + d + NZ, NZ)

    def at_y(d):
        return lax.rem(y + d, NY)

    def remote(src, dst, send, recv, **where):
        return pltpu.make_async_remote_copy(
            src_ref=src, dst_ref=dst, send_sem=send, recv_sem=recv, device_id=where, device_id_type=MESH
        )

    def ring(way, s):
        block = hidden_ref.at[at_z(-s if way == 0 else s)]
        return remote(
            block, block, ring_send.at[way, s], ring_recv.at[way, s], z=at_z(1 if way == 0 else -1)
        )

    def push(d):
        return remote(
            rows_ref.at[at_z(d)], group_ref.at[y, z], x_send.at[d], x_recv.at[d], z=at_z(d)
        )

    def forward(d, e):
        block = group_ref.at[y, at_z(-d)]
        return remote(block, block, f_send.at[d, e], f_recv.at[d, e], y=at_y(e))

    def relay(d, way):
        from_y, cut = (at_y(3), pl.ds(0, CUT)) if way == 0 else (at_y(1), pl.ds(CUT, 2 * CAP - CUT))
        block = group_ref.at[from_y, at_z(-d), cut]
        return remote(block, block, r_send.at[way, d], r_recv.at[way, d], y=at_y(1 if way == 0 else 3))

    def latent_y(d):
        return remote(part_ref.at[at_y(d)], crossed.at[d - 1], y_send.at[d], y_recv.at[d], y=at_y(d))

    mid = part_ref.shape[1] // 2

    def latent_out(way):
        return remote(
            part_ref.at[at_y(2), pl.ds(way * mid, mid)], middle.at[way],
            m_send.at[0, way], m_recv.at[0, way], y=at_y(1 if way == 0 else 3),
        )

    def latent_on(way):
        return remote(
            middle.at[way], crossed.at[1, pl.ds(way * mid, mid)],
            m_send.at[1, way], m_recv.at[1, way], y=at_y(1 if way == 0 else 3),
        )

    def latent_z(way, s):
        return remote(
            carry.at[way, s], landed.at[way, s], l_send.at[way, s], l_recv.at[way, s],
            z=at_z(1 if way == 0 else -1),
        )

    def term(way, s):
        return summed[at_z(NZ // 2 - s if way == 0 else s - NZ // 2 + 1)]

    def each(first, last, step):
        lax.fori_loop(first, last, lambda i, _: (step(i), 0)[1], 0)

    barrier = pltpu.get_barrier_semaphore()
    each(1, NZ, lambda d: pl.semaphore_signal(barrier, inc=1, device_id={"z": at_z(d)}, device_id_type=MESH))
    each(1, NY, lambda d: pl.semaphore_signal(barrier, inc=1, device_id={"y": at_y(d)}, device_id_type=MESH))
    pl.semaphore_wait(barrier, NZ + NY - 2)

    keep = pltpu.make_async_copy(hid_ref, hidden_ref.at[z], local.at[0])
    own = pltpu.make_async_copy(rows_ref.at[z], group_ref.at[y, z], local.at[1])
    keep.start()
    own.start()
    keep.wait()
    ring(0, 0).start()
    ring(1, 0).start()
    for way in range(2):
        latent_out(way).start()
    latent_y(1).start()
    latent_y(3).start()
    push(NZ // 2).start()
    own.wait()

    def spread(d):
        forward(d, 1).start()
        forward(d, 3).start()

    def relays(d):
        forward(d, 1).wait_recv()
        relay(d, 0).start()
        forward(d, 3).wait_recv()
        relay(d, 1).start()

    spread(0)
    half = NZ // 2
    last = half - 1

    def turn(s):
        ring(0, s - 1).wait_recv()
        ring(0, s).start()
        ring(1, s - 1).wait_recv()

    def send(s):
        push(half - s).start()
        push(half + s).start()

    def take(s):
        push(half - s).wait_recv()
        spread(half - s)
        push(half + s).wait_recv()
        spread(half + s)

    def pass_on(s):
        relays(half - s)
        relays(half + s)

    def both(s):
        turn(s)
        ring(1, s).start()
        send(s)
        take(s - 1)
        pass_on(s - 2)

    def add_on(way, s):
        latent_z(way, s - 1).wait_recv()
        carry[way, s] = landed[way, s - 1] + term(way, s)
        latent_z(way, s).start()

    turn(1)
    ring(1, 1).start()
    send(1)
    for way in range(2):
        latent_out(way).wait_recv()
        latent_on(way).start()
    push(half).wait_recv()
    spread(half)
    relays(0)
    turn(2)
    ring(1, 2).start()
    send(2)
    take(1)
    relays(half)
    both(3)
    latent_y(1).wait_recv()
    latent_y(3).wait_recv()
    for way in range(2):
        latent_on(way).wait_recv()
    summed[...] = (part_ref[y] + crossed[0] + crossed[1] + crossed[2]).reshape(summed.shape)
    for way in range(2):
        carry[way, 0] = term(way, 0)
    both(4)
    for way in range(2):
        latent_z(way, 0).start()

    def all_three(s):
        both(s)
        add_on(0, s - 4)
        add_on(1, s - 4)

    each(5, last, all_three)
    turn(last)
    send(last)
    take(last - 1)
    add_on(0, 3)
    add_on(1, 3)
    pass_on(last - 2)
    take(last)
    pass_on(last - 1)
    add_on(0, 4)
    add_on(1, 4)
    pass_on(last)

    def add_both(s):
        add_on(0, s)
        add_on(1, s)

    each(5, last, add_both)
    add_on(0, last)
    latent_z(1, last - 1).wait_recv()
    latent_z(0, last).wait_recv()
    total_ref[...] = summed[z] + landed[0, last] + landed[1, last - 1]
    ring(0, last).wait_recv()

    def drain(d):
        forward(d, 1).wait_send()
        forward(d, 3).wait_send()
        relay(d, 0).wait()
        relay(d, 1).wait()

    each(0, NZ, drain)

    def drain_rings(s):
        ring(0, s).wait_send()
        ring(1, s).wait_send()
        latent_z(0, s).wait_send()
        latent_z(1, s).wait_send()

    each(0, last, drain_rings)
    ring(0, last).wait_send()
    latent_z(0, last).wait_send()
    each(1, NZ, lambda d: push(d).wait_send())
    for way in range(2):
        latent_out(way).wait_send()
        latent_on(way).wait_send()
    latent_y(1).wait_send()
    latent_y(3).wait_send()


def exchange(rows, hidden_part, partial):
    whole = pl.BlockSpec(memory_space=pltpu.VMEM)
    wide, lat = partial.shape[1] // NZ, partial.shape[2]
    dma = pltpu.SemaphoreType.DMA
    return pl.pallas_call(
        exchange_kernel,
        out_shape=(
            jax.ShapeDtypeStruct((NY, NZ, 2 * CAP, PAD), jnp.bfloat16),
            jax.ShapeDtypeStruct((NZ, 2 * CAP, EXTRA * PAD), jnp.bfloat16),
            jax.ShapeDtypeStruct((wide, lat), jnp.float32),
        ),
        in_specs=[whole] * 3,
        out_specs=(whole,) * 3,
        scratch_shapes=[
            pltpu.VMEM((NY - 1, NZ * wide, lat), jnp.float32),
            pltpu.VMEM((2, NZ * wide // 2, lat), jnp.float32),
            pltpu.VMEM((NZ, wide, lat), jnp.float32),
            pltpu.VMEM((2, NZ // 2, wide, lat), jnp.float32),
            pltpu.VMEM((2, NZ // 2, wide, lat), jnp.float32),
            dma((2,)),
            dma((2, NZ // 2)),
            dma((2, NZ // 2)),
            dma((NZ,)),
            dma((NZ,)),
            dma((NZ, NY)),
            dma((NZ, NY)),
            dma((2, NZ)),
            dma((2, NZ)),
            dma((NY,)),
            dma((NY,)),
            dma((2, 2)),
            dma((2, 2)),
            dma((2, NZ // 2)),
            dma((2, NZ // 2)),
        ],
        compiler_params=pltpu.CompilerParams(collective_id=0, has_side_effects=True),
        name="exchange",
    )(rows, hidden_part, partial)


def on_device(
    attn_input,
    latent_grad,
    latent_param,
    latent_first,
    latent_second,
    expert_input,
    hidden_grad,
    counts,
    block_owner,
    expert_param,
    expert_first,
    expert_second,
):
    z, y = lax.axis_index("z"), lax.axis_index("y")
    expert = lax.axis_index("expert")
    position = z * NY + y
    own_counts = lax.dynamic_slice_in_dim(counts, expert, 1, 1)[:, 0]
    count = lax.dynamic_index_in_dim(own_counts, position, 0, keepdims=False)
    offset = jnp.where(y % 2 == 1, CAP - count, 0)
    blocks = jnp.arange(N_DP, dtype=jnp.int32)
    holder = jnp.sum(jnp.where(block_owner[0][:, None] == blocks[None, :], blocks[:, None], 0), axis=0)
    packed = pack(holder, jnp.stack([count, offset]), expert_input[0], hidden_grad[0])

    crossed = lax.all_to_all(packed, "y", split_axis=0, concat_axis=0, tiled=True)
    rows, hidden_part = merge(crossed)
    feat = attn_input.shape[1]
    shard = feat // N_DP
    wide = 16
    source = lax.broadcasted_iota(jnp.int32, (feat, N_DP * wide), 0)
    target = lax.broadcasted_iota(jnp.int32, (feat, N_DP * wide), 1)
    owner = (target // wide % NZ) * NY + target // wide // NZ
    spread = (source == owner * shard + target % wide) & (target % wide < shard)
    columns = jnp.dot(
        attn_input, spread.astype(jnp.bfloat16), preferred_element_type=jnp.bfloat16
    )
    partial = lax.dot_general(
        columns, latent_grad, (((0,), (0,)), ((), ())), preferred_element_type=jnp.float32
    )
    group, hidden, grad_latent = exchange(
        rows.reshape(NZ, 2 * CAP, PAD), hidden_part, partial.reshape(NY, NZ * wide, -1)
    )
    group = group.reshape(NY, NZ * 2 * CAP, PAD)
    hidden = hidden.reshape(NZ * 2 * CAP, EXTRA * PAD)
    quarter = jnp.stack(
        [
            lax.dot_general(
                group[i], hidden, (((0,), (0,)), ((), ())), preferred_element_type=jnp.float32
            )[:SHARD]
            for i in range(NY)
        ]
    )
    grad_expert = lax.all_to_all(quarter, "y", split_axis=0, concat_axis=0, tiled=True)
    grad_expert = grad_expert.transpose(1, 0, 2).reshape(1, SHARD, FFE)
    expert_new = adam_step(grad_expert, expert_param, expert_first, expert_second)

    latent_new = adam_step(grad_latent[None, :shard], latent_param, latent_first, latent_second)
    return (*latent_new, *expert_new)


def solution(mesh):
    grid = Mesh(mesh.devices.reshape(NZ, NY, -1), ("z", "y", "expert"))
    dp = ("z", "y")
    sharded = P("expert", dp, None)
    return jax.shard_map(
        on_device,
        mesh=grid,
        in_specs=(
            P(dp, "expert"),
            P(dp, None),
            sharded,
            sharded,
            sharded,
            sharded,
            sharded,
            P(),
            P("expert", None),
            sharded,
            sharded,
            sharded,
        ),
        out_specs=(sharded,) * 6,
        check_vma=False,
    )
```

```python
import jax
import jax.numpy as jnp
from jax import lax
from jax.experimental import pallas as pl
from jax.experimental.pallas import tpu as pltpu
from jax.sharding import Mesh, PartitionSpec as P

STEP = 20
FIRST_BETA = 0.9
SECOND_BETA = 0.95
LEARNING_RATE = 0.1
WEIGHT_DECAY = 0.5
EPSILON = 1e-08

NZ, NY, CAP, SHARD, D, FFE = 16, 4, 88, 112, 7168, 1024
PAD = 128
N_DP = NZ * NY
EXTRA = FFE // NY // PAD
PARTS = NZ + EXTRA


def adam_step(gradient, weights, moment_one, moment_two):
    first_new = FIRST_BETA * moment_one + (1.0 - FIRST_BETA) * gradient
    second_new = SECOND_BETA * moment_two + (1.0 - SECOND_BETA) * gradient * gradient
    mean_hat = first_new / (1.0 - FIRST_BETA**STEP)
    scale_hat = second_new / (1.0 - SECOND_BETA**STEP)
    update = mean_hat / (jnp.sqrt(scale_hat) + EPSILON) + WEIGHT_DECAY * weights
    return (weights - LEARNING_RATE * update, first_new, second_new)


def pack_kernel(holder_ref, place_ref, x_ref, h_ref, out_ref):
    count, offset = place_ref[0], place_ref[1]
    row = lax.broadcasted_iota(jnp.int32, (CAP, CAP), 0)
    slot = lax.broadcasted_iota(jnp.int32, (CAP, CAP), 1)
    select = ((slot < count) & (row == slot + offset)).astype(jnp.float32).astype(jnp.bfloat16)
    source = lax.broadcasted_iota(jnp.int32, (2 * PAD, PAD), 0)
    lane = lax.broadcasted_iota(jnp.int32, (2 * PAD, PAD), 1)
    y = pl.program_id(0)
    for z in range(NZ):
        first = holder_ref[z * NY + y] * SHARD
        base = jnp.minimum(first // PAD, D // PAD - 2) * PAD
        window = x_ref[:, pl.ds(pl.multiple_of(base, PAD), 2 * PAD)]
        pick = ((source == lane + (first - base)) & (lane < SHARD)).astype(jnp.float32).astype(jnp.bfloat16)
        block = jnp.dot(window, pick, preferred_element_type=jnp.float32).astype(jnp.bfloat16)
        out_ref[0, z] = jnp.dot(select, block, preferred_element_type=jnp.float32).astype(jnp.bfloat16)
    for part in range(EXTRA):
        columns = pl.ds(pl.multiple_of((y * EXTRA + part) * PAD, PAD), PAD)
        out_ref[0, NZ + part] = jnp.dot(
            select, h_ref[:, columns], preferred_element_type=jnp.float32
        ).astype(jnp.bfloat16)


def pack(holder, place, rows, hidden):
    return pl.pallas_call(
        pack_kernel,
        out_shape=jax.ShapeDtypeStruct((NY, PARTS, CAP, PAD), jnp.bfloat16),
        grid_spec=pltpu.PrefetchScalarGridSpec(
            num_scalar_prefetch=2,
            grid=(NY,),
            in_specs=[
                pl.BlockSpec((CAP, D), lambda i, *_: (0, 0)),
                pl.BlockSpec((CAP, FFE), lambda i, *_: (0, 0)),
            ],
            out_specs=pl.BlockSpec((1, PARTS, CAP, PAD), lambda i, *_: (i, 0, 0, 0)),
        ),
        cost_estimate=pl.CostEstimate(
            flops=2 * N_DP * CAP * PAD * 400, bytes_accessed=3_000_000, transcendentals=0
        ),
        name="pack",
    )(holder, place, rows, hidden)


MESH = pl.DeviceIdType.MESH


def exchange_kernel(
    packed_ref, part_ref, group_ref, hidden_ref, total_ref, arr, across, rows_ref, hid_ref, crossed, middle, summed, carry, landed,
    local, ring_send, ring_recv, x_send, x_recv, f_send, f_recv, r_send, r_recv, y_send, y_recv,
    m_send, m_recv, l_send, l_recv, a_send, a_recv, b_send, b_recv,
):
    z, y = lax.axis_index("z"), lax.axis_index("y")

    def at_z(d):
        return lax.rem(z + d + NZ, NZ)

    def at_y(d):
        return lax.rem(y + d, NY)

    def remote(src, dst, send, recv, **where):
        return pltpu.make_async_remote_copy(
            src_ref=src, dst_ref=dst, send_sem=send, recv_sem=recv, device_id=where, device_id_type=MESH
        )

    def ring(way, s):
        block = hidden_ref.at[at_z(-s if way == 0 else s)]
        return remote(
            block, block, ring_send.at[way, s], ring_recv.at[way, s], z=at_z(1 if way == 0 else -1)
        )

    def push(d):
        return remote(
            rows_ref.at[at_z(d)], group_ref.at[y, z], x_send.at[d], x_recv.at[d], z=at_z(d)
        )

    def forward(d, e):
        block = group_ref.at[y, at_z(-d)]
        return remote(block, block, f_send.at[d, e], f_recv.at[d, e], y=at_y(e))

    def relay(d, way):
        block = group_ref.at[at_y(3 if way == 0 else 1), at_z(-d), way]
        return remote(block, block, r_send.at[way, d], r_recv.at[way, d], y=at_y(1 if way == 0 else 3))

    def cross(d):
        return remote(packed_ref.at[at_y(d)], arr.at[d - 1], a_send.at[d], a_recv.at[d], y=at_y(d))

    some = PARTS // 2

    def cross_out(way):
        return remote(
            packed_ref.at[at_y(2), pl.ds(way * some, some)], across.at[way],
            b_send.at[0, way], b_recv.at[0, way], y=at_y(1 if way == 0 else 3),
        )

    def cross_on(way):
        return remote(
            across.at[way], arr.at[1, pl.ds(way * some, some)],
            b_send.at[1, way], b_recv.at[1, way], y=at_y(1 if way == 0 else 3),
        )

    def latent_y(d):
        return remote(part_ref.at[at_y(d)], crossed.at[d - 1], y_send.at[d], y_recv.at[d], y=at_y(d))

    mid = part_ref.shape[1] // 2

    def latent_out(way):
        return remote(
            part_ref.at[at_y(2), pl.ds(way * mid, mid)], middle.at[way],
            m_send.at[0, way], m_recv.at[0, way], y=at_y(1 if way == 0 else 3),
        )

    def latent_on(way):
        return remote(
            middle.at[way], crossed.at[1, pl.ds(way * mid, mid)],
            m_send.at[1, way], m_recv.at[1, way], y=at_y(1 if way == 0 else 3),
        )

    def latent_z(way, s):
        return remote(
            carry.at[way, s], landed.at[way, s], l_send.at[way, s], l_recv.at[way, s],
            z=at_z(1 if way == 0 else -1),
        )

    def term(way, s):
        return summed[at_z(NZ // 2 - s if way == 0 else s - NZ // 2 + 1)]

    def each(first, last, step):
        lax.fori_loop(first, last, lambda i, _: (step(i), 0)[1], 0)

    barrier = pltpu.get_barrier_semaphore()
    each(1, NZ, lambda d: pl.semaphore_signal(barrier, inc=1, device_id={"z": at_z(d)}, device_id_type=MESH))
    each(1, NY, lambda d: pl.semaphore_signal(barrier, inc=1, device_id={"y": at_y(d)}, device_id_type=MESH))
    pl.semaphore_wait(barrier, NZ + NY - 2)

    mine = pltpu.make_async_copy(packed_ref.at[y], arr.at[NY - 1], local.at[2])
    mine.start()
    for way in range(2):
        cross_out(way).start()
    cross(1).start()
    cross(3).start()
    for way in range(2):
        cross_out(way).wait_recv()
        cross_on(way).start()
    for way in range(2):
        latent_out(way).start()
    latent_y(1).start()
    latent_y(3).start()
    mine.wait()
    cross(1).wait_recv()
    cross(3).wait_recv()
    for way in range(2):
        cross_on(way).wait_recv()

    slots = [lax.rem(y - source + 2 * NY - 1, NY) for source in range(NY)]
    for p in range(2):
        one, two = slots[2 * p], slots[2 * p + 1]
        for part in range(EXTRA):
            hid_ref[p * CAP : (p + 1) * CAP, part * PAD : (part + 1) * PAD] = (
                arr[one, NZ + part] + arr[two, NZ + part]
            )

    keep = pltpu.make_async_copy(hid_ref, hidden_ref.at[z], local.at[0])

    def fill(i):
        for p in range(2):
            rows_ref[i, p] = arr[slots[2 * p], i] + arr[slots[2 * p + 1], i]

    each(0, NZ, fill)
    own = pltpu.make_async_copy(rows_ref.at[z], group_ref.at[y, z], local.at[1])
    keep.start()
    own.start()
    keep.wait()
    ring(0, 0).start()
    ring(1, 0).start()
    push(NZ // 2).start()
    own.wait()

    def spread(d):
        forward(d, 1).start()
        forward(d, 3).start()

    def relays(d):
        forward(d, 1).wait_recv()
        relay(d, 0).start()
        forward(d, 3).wait_recv()
        relay(d, 1).start()

    spread(0)
    half = NZ // 2
    last = half - 1

    def turn(s):
        ring(0, s - 1).wait_recv()
        ring(0, s).start()
        ring(1, s - 1).wait_recv()

    def send(s):
        push(half - s).start()
        push(half + s).start()

    def take(s):
        push(half - s).wait_recv()
        spread(half - s)
        push(half + s).wait_recv()
        spread(half + s)

    def pass_on(s):
        relays(half - s)
        relays(half + s)

    def both(s):
        turn(s)
        ring(1, s).start()
        send(s)
        take(s - 1)
        pass_on(s - 2)

    def add_on(way, s):
        latent_z(way, s - 1).wait_recv()
        carry[way, s] = landed[way, s - 1] + term(way, s)
        latent_z(way, s).start()

    turn(1)
    ring(1, 1).start()
    send(1)
    for way in range(2):
        latent_out(way).wait_recv()
        latent_on(way).start()
    push(half).wait_recv()
    spread(half)
    relays(0)
    turn(2)
    ring(1, 2).start()
    send(2)
    take(1)
    relays(half)
    both(3)
    latent_y(1).wait_recv()
    latent_y(3).wait_recv()
    for way in range(2):
        latent_on(way).wait_recv()
    summed[...] = (part_ref[y] + crossed[0] + crossed[1] + crossed[2]).reshape(summed.shape)
    for way in range(2):
        carry[way, 0] = term(way, 0)
    both(4)
    for way in range(2):
        latent_z(way, 0).start()

    def all_three(s):
        both(s)
        add_on(0, s - 4)
        add_on(1, s - 4)

    each(5, last, all_three)
    turn(last)
    send(last)
    take(last - 1)
    add_on(0, 3)
    add_on(1, 3)
    pass_on(last - 2)
    take(last)
    pass_on(last - 1)
    add_on(0, 4)
    add_on(1, 4)
    pass_on(last)

    def add_both(s):
        add_on(0, s)
        add_on(1, s)

    each(5, last, add_both)
    add_on(0, last)
    latent_z(1, last - 1).wait_recv()
    latent_z(0, last).wait_recv()
    total_ref[...] = summed[z] + landed[0, last] + landed[1, last - 1]
    ring(0, last).wait_recv()

    def drain(d):
        forward(d, 1).wait_send()
        forward(d, 3).wait_send()
        relay(d, 0).wait()
        relay(d, 1).wait()

    each(0, NZ, drain)

    def drain_rings(s):
        ring(0, s).wait_send()
        ring(1, s).wait_send()
        latent_z(0, s).wait_send()
        latent_z(1, s).wait_send()

    each(0, last, drain_rings)
    ring(0, last).wait_send()
    latent_z(0, last).wait_send()
    each(1, NZ, lambda d: push(d).wait_send())
    cross(1).wait_send()
    cross(3).wait_send()
    for way in range(2):
        cross_out(way).wait_send()
        cross_on(way).wait_send()
    for way in range(2):
        latent_out(way).wait_send()
        latent_on(way).wait_send()
    latent_y(1).wait_send()
    latent_y(3).wait_send()


def exchange(packed, partial):
    whole = pl.BlockSpec(memory_space=pltpu.VMEM)
    wide, lat = partial.shape[1] // NZ, partial.shape[2]
    dma = pltpu.SemaphoreType.DMA
    return pl.pallas_call(
        exchange_kernel,
        out_shape=(
            jax.ShapeDtypeStruct((NY, NZ, 2, CAP, PAD), jnp.bfloat16),
            jax.ShapeDtypeStruct((NZ, 2 * CAP, EXTRA * PAD), jnp.bfloat16),
            jax.ShapeDtypeStruct((wide, lat), jnp.float32),
        ),
        in_specs=[whole] * 2,
        out_specs=(whole,) * 3,
        scratch_shapes=[
            pltpu.VMEM((NY, PARTS, CAP, PAD), jnp.bfloat16),
            pltpu.VMEM((2, PARTS // 2, CAP, PAD), jnp.bfloat16),
            pltpu.VMEM((NZ, 2, CAP, PAD), jnp.bfloat16),
            pltpu.VMEM((2 * CAP, EXTRA * PAD), jnp.bfloat16),
            pltpu.VMEM((NY - 1, NZ * wide, lat), jnp.float32),
            pltpu.VMEM((2, NZ * wide // 2, lat), jnp.float32),
            pltpu.VMEM((NZ, wide, lat), jnp.float32),
            pltpu.VMEM((2, NZ // 2, wide, lat), jnp.float32),
            pltpu.VMEM((2, NZ // 2, wide, lat), jnp.float32),
            dma((3,)),
            dma((2, NZ // 2)),
            dma((2, NZ // 2)),
            dma((NZ,)),
            dma((NZ,)),
            dma((NZ, NY)),
            dma((NZ, NY)),
            dma((2, NZ)),
            dma((2, NZ)),
            dma((NY,)),
            dma((NY,)),
            dma((2, 2)),
            dma((2, 2)),
            dma((2, NZ // 2)),
            dma((2, NZ // 2)),
            dma((NY,)),
            dma((NY,)),
            dma((2, 2)),
            dma((2, 2)),
        ],
        compiler_params=pltpu.CompilerParams(collective_id=0, has_side_effects=True),
        name="exchange",
    )(packed, partial)


def on_device(
    attn_input,
    latent_grad,
    latent_param,
    latent_first,
    latent_second,
    expert_input,
    hidden_grad,
    counts,
    block_owner,
    expert_param,
    expert_first,
    expert_second,
):
    z, y = lax.axis_index("z"), lax.axis_index("y")
    expert = lax.axis_index("expert")
    position = z * NY + y
    own_counts = lax.dynamic_slice_in_dim(counts, expert, 1, 1)[:, 0]
    count = lax.dynamic_index_in_dim(own_counts, position, 0, keepdims=False)
    offset = jnp.where(y % 2 == 1, CAP - count, 0)
    blocks = jnp.arange(N_DP, dtype=jnp.int32)
    holder = jnp.sum(jnp.where(block_owner[0][:, None] == blocks[None, :], blocks[:, None], 0), axis=0)
    packed = pack(holder, jnp.stack([count, offset]), expert_input[0], hidden_grad[0])

    feat = attn_input.shape[1]
    shard = feat // N_DP
    wide = 16
    source = lax.broadcasted_iota(jnp.int32, (feat, N_DP * wide), 0)
    target = lax.broadcasted_iota(jnp.int32, (feat, N_DP * wide), 1)
    owner = (target // wide % NZ) * NY + target // wide // NZ
    spread = (source == owner * shard + target % wide) & (target % wide < shard)
    columns = jnp.dot(
        attn_input, spread.astype(jnp.bfloat16), preferred_element_type=jnp.bfloat16
    )
    partial = lax.dot_general(
        columns, latent_grad, (((0,), (0,)), ((), ())), preferred_element_type=jnp.float32
    )
    group, hidden, grad_latent = exchange(packed, partial.reshape(NY, NZ * wide, -1))
    group = group.reshape(NY, NZ * 2 * CAP, PAD)
    hidden = hidden.reshape(NZ * 2 * CAP, EXTRA * PAD)
    quarter = jnp.stack(
        [
            lax.dot_general(
                group[i], hidden, (((0,), (0,)), ((), ())), preferred_element_type=jnp.float32
            )[:SHARD]
            for i in range(NY)
        ]
    )
    grad_expert = lax.all_to_all(quarter, "y", split_axis=0, concat_axis=0, tiled=True)
    grad_expert = grad_expert.transpose(1, 0, 2).reshape(1, SHARD, FFE)
    expert_new = adam_step(grad_expert, expert_param, expert_first, expert_second)

    latent_new = adam_step(grad_latent[None, :shard], latent_param, latent_first, latent_second)
    return (*latent_new, *expert_new)


def solution(mesh):
    grid = Mesh(mesh.devices.reshape(NZ, NY, -1), ("z", "y", "expert"))
    dp = ("z", "y")
    sharded = P("expert", dp, None)
    return jax.shard_map(
        on_device,
        mesh=grid,
        in_specs=(
            P(dp, "expert"),
            P(dp, None),
            sharded,
            sharded,
            sharded,
            sharded,
            sharded,
            P(),
            P("expert", None),
            sharded,
            sharded,
            sharded,
        ),
        out_specs=(sharded,) * 6,
        check_vma=False,
    )
```

```python
import jax
import jax.numpy as jnp
from jax import lax
from jax.experimental import pallas as pl
from jax.experimental.pallas import tpu as pltpu
from jax.sharding import Mesh, PartitionSpec as P

STEP = 20
FIRST_BETA = 0.9
SECOND_BETA = 0.95
LEARNING_RATE = 0.1
WEIGHT_DECAY = 0.5
EPSILON = 1e-08

NZ, NY, CAP, SHARD, D, FFE = 16, 4, 88, 112, 7168, 1024
PAD = 128
N_DP = NZ * NY
EXTRA = FFE // NY // PAD
PARTS = NZ + EXTRA


def adam_step(gradient, weights, moment_one, moment_two):
    first_new = FIRST_BETA * moment_one + (1.0 - FIRST_BETA) * gradient
    second_new = SECOND_BETA * moment_two + (1.0 - SECOND_BETA) * gradient * gradient
    mean_hat = first_new / (1.0 - FIRST_BETA**STEP)
    scale_hat = second_new / (1.0 - SECOND_BETA**STEP)
    update = mean_hat / (jnp.sqrt(scale_hat) + EPSILON) + WEIGHT_DECAY * weights
    return (weights - LEARNING_RATE * update, first_new, second_new)


def pack_kernel(owner_ref, counts_ref, x_ref, h_ref, out_ref, holder_ref):
    own_y = lax.axis_index("y")
    count = counts_ref[lax.axis_index("expert"), lax.axis_index("z") * NY + own_y]
    offset = jnp.where(lax.rem(own_y, 2) == 1, CAP - count, 0)

    @pl.when(pl.program_id(0) == 0)
    def _():
        for b in range(N_DP):
            holder_ref[owner_ref[0, b]] = b

    row = lax.broadcasted_iota(jnp.int32, (CAP, CAP), 0)
    slot = lax.broadcasted_iota(jnp.int32, (CAP, CAP), 1)
    select = ((slot < count) & (row == slot + offset)).astype(jnp.float32).astype(jnp.bfloat16)
    source = lax.broadcasted_iota(jnp.int32, (2 * PAD, PAD), 0)
    lane = lax.broadcasted_iota(jnp.int32, (2 * PAD, PAD), 1)
    y = pl.program_id(0)
    for z in range(NZ):
        first = holder_ref[z * NY + y] * SHARD
        base = jnp.minimum(first // PAD, D // PAD - 2) * PAD
        window = x_ref[:, pl.ds(pl.multiple_of(base, PAD), 2 * PAD)]
        pick = ((source == lane + (first - base)) & (lane < SHARD)).astype(jnp.float32).astype(jnp.bfloat16)
        block = jnp.dot(window, pick, preferred_element_type=jnp.float32).astype(jnp.bfloat16)
        out_ref[0, z] = jnp.dot(select, block, preferred_element_type=jnp.float32).astype(jnp.bfloat16)
    for part in range(EXTRA):
        columns = pl.ds(pl.multiple_of((y * EXTRA + part) * PAD, PAD), PAD)
        out_ref[0, NZ + part] = jnp.dot(
            select, h_ref[:, columns], preferred_element_type=jnp.float32
        ).astype(jnp.bfloat16)


def pack(owner, counts, rows, hidden):
    return pl.pallas_call(
        pack_kernel,
        out_shape=jax.ShapeDtypeStruct((NY, PARTS, CAP, PAD), jnp.bfloat16),
        grid_spec=pltpu.PrefetchScalarGridSpec(
            num_scalar_prefetch=2,
            grid=(NY,),
            in_specs=[
                pl.BlockSpec((CAP, D), lambda i, *_: (0, 0)),
                pl.BlockSpec((CAP, FFE), lambda i, *_: (0, 0)),
            ],
            out_specs=pl.BlockSpec((1, PARTS, CAP, PAD), lambda i, *_: (i, 0, 0, 0)),
            scratch_shapes=[pltpu.SMEM((N_DP,), jnp.int32)],
        ),
        cost_estimate=pl.CostEstimate(
            flops=2 * N_DP * CAP * PAD * 400, bytes_accessed=3_000_000, transcendentals=0
        ),
        name="pack",
    )(owner, counts, rows, hidden)


MESH = pl.DeviceIdType.MESH


def exchange_kernel(
    packed_ref, part_ref, group_ref, hidden_ref, total_ref, arr, across, rows_ref, hid_ref, crossed, middle, summed, carry, landed,
    local, ring_send, ring_recv, x_send, x_recv, f_send, f_recv, r_send, r_recv, y_send, y_recv,
    m_send, m_recv, l_send, l_recv, a_send, a_recv, b_send, b_recv,
):
    z, y = lax.axis_index("z"), lax.axis_index("y")

    def at_z(d):
        return lax.rem(z + d + NZ, NZ)

    def at_y(d):
        return lax.rem(y + d, NY)

    def remote(src, dst, send, recv, **where):
        return pltpu.make_async_remote_copy(
            src_ref=src, dst_ref=dst, send_sem=send, recv_sem=recv, device_id=where, device_id_type=MESH
        )

    def ring(way, s):
        block = hidden_ref.at[at_z(-s if way == 0 else s)]
        return remote(
            block, block, ring_send.at[way, s], ring_recv.at[way, s], z=at_z(1 if way == 0 else -1)
        )

    def push(d):
        return remote(
            rows_ref.at[at_z(d)], group_ref.at[y, z], x_send.at[d], x_recv.at[d], z=at_z(d)
        )

    def forward(d, e):
        block = group_ref.at[y, at_z(-d)]
        return remote(block, block, f_send.at[d, e], f_recv.at[d, e], y=at_y(e))

    def relay(d, way):
        block = group_ref.at[at_y(3 if way == 0 else 1), at_z(-d), way]
        return remote(block, block, r_send.at[way, d], r_recv.at[way, d], y=at_y(1 if way == 0 else 3))

    def cross(d):
        return remote(packed_ref.at[at_y(d)], arr.at[d - 1], a_send.at[d], a_recv.at[d], y=at_y(d))

    some = PARTS // 2

    def cross_out(way):
        return remote(
            packed_ref.at[at_y(2), pl.ds(way * some, some)], across.at[way],
            b_send.at[0, way], b_recv.at[0, way], y=at_y(1 if way == 0 else 3),
        )

    def cross_on(way):
        return remote(
            across.at[way], arr.at[1, pl.ds(way * some, some)],
            b_send.at[1, way], b_recv.at[1, way], y=at_y(1 if way == 0 else 3),
        )

    def latent_y(d):
        return remote(part_ref.at[at_y(d)], crossed.at[d - 1], y_send.at[d], y_recv.at[d], y=at_y(d))

    mid = part_ref.shape[1] // 2

    def latent_out(way):
        return remote(
            part_ref.at[at_y(2), pl.ds(way * mid, mid)], middle.at[way],
            m_send.at[0, way], m_recv.at[0, way], y=at_y(1 if way == 0 else 3),
        )

    def latent_on(way):
        return remote(
            middle.at[way], crossed.at[1, pl.ds(way * mid, mid)],
            m_send.at[1, way], m_recv.at[1, way], y=at_y(1 if way == 0 else 3),
        )

    def latent_z(way, s):
        return remote(
            carry.at[way, s], landed.at[way, s], l_send.at[way, s], l_recv.at[way, s],
            z=at_z(1 if way == 0 else -1),
        )

    def term(way, s):
        return summed[at_z(NZ // 2 - s if way == 0 else s - NZ // 2 + 1)]

    def each(first, last, step):
        lax.fori_loop(first, last, lambda i, _: (step(i), 0)[1], 0)

    barrier = pltpu.get_barrier_semaphore()
    each(1, NZ, lambda d: pl.semaphore_signal(barrier, inc=1, device_id={"z": at_z(d)}, device_id_type=MESH))
    each(1, NY, lambda d: pl.semaphore_signal(barrier, inc=1, device_id={"y": at_y(d)}, device_id_type=MESH))
    pl.semaphore_wait(barrier, NZ + NY - 2)

    mine = pltpu.make_async_copy(packed_ref.at[y], arr.at[NY - 1], local.at[2])
    mine.start()
    for way in range(2):
        cross_out(way).start()
    cross(1).start()
    cross(3).start()
    for way in range(2):
        cross_out(way).wait_recv()
        cross_on(way).start()
    for way in range(2):
        latent_out(way).start()
    latent_y(1).start()
    latent_y(3).start()
    mine.wait()
    cross(1).wait_recv()
    cross(3).wait_recv()
    for way in range(2):
        cross_on(way).wait_recv()

    slots = [lax.rem(y - source + 2 * NY - 1, NY) for source in range(NY)]
    for p in range(2):
        one, two = slots[2 * p], slots[2 * p + 1]
        for part in range(EXTRA):
            hid_ref[p * CAP : (p + 1) * CAP, part * PAD : (part + 1) * PAD] = (
                arr[one, NZ + part] + arr[two, NZ + part]
            )

    keep = pltpu.make_async_copy(hid_ref, hidden_ref.at[z], local.at[0])

    def fill(i):
        for p in range(2):
            rows_ref[i, p] = arr[slots[2 * p], i] + arr[slots[2 * p + 1], i]

    each(0, NZ, fill)
    own = pltpu.make_async_copy(rows_ref.at[z], group_ref.at[y, z], local.at[1])
    keep.start()
    own.start()
    keep.wait()
    ring(0, 0).start()
    ring(1, 0).start()
    push(NZ // 2).start()
    own.wait()

    def spread(d):
        forward(d, 1).start()
        forward(d, 3).start()

    def relays(d):
        forward(d, 1).wait_recv()
        relay(d, 0).start()
        forward(d, 3).wait_recv()
        relay(d, 1).start()

    spread(0)
    half = NZ // 2
    last = half - 1

    def turn(s):
        ring(0, s - 1).wait_recv()
        ring(0, s).start()
        ring(1, s - 1).wait_recv()

    def send(s):
        push(half - s).start()
        push(half + s).start()

    def take(s):
        push(half - s).wait_recv()
        spread(half - s)
        push(half + s).wait_recv()
        spread(half + s)

    def pass_on(s):
        relays(half - s)
        relays(half + s)

    def both(s):
        turn(s)
        ring(1, s).start()
        send(s)
        take(s - 1)
        pass_on(s - 2)

    def add_on(way, s):
        latent_z(way, s - 1).wait_recv()
        carry[way, s] = landed[way, s - 1] + term(way, s)
        latent_z(way, s).start()

    turn(1)
    ring(1, 1).start()
    send(1)
    for way in range(2):
        latent_out(way).wait_recv()
        latent_on(way).start()
    push(half).wait_recv()
    spread(half)
    relays(0)
    turn(2)
    ring(1, 2).start()
    send(2)
    take(1)
    relays(half)
    both(3)
    latent_y(1).wait_recv()
    latent_y(3).wait_recv()
    for way in range(2):
        latent_on(way).wait_recv()
    summed[...] = (part_ref[y] + crossed[0] + crossed[1] + crossed[2]).reshape(summed.shape)
    for way in range(2):
        carry[way, 0] = term(way, 0)
    both(4)
    for way in range(2):
        latent_z(way, 0).start()

    def all_three(s):
        both(s)
        add_on(0, s - 4)
        add_on(1, s - 4)

    each(5, last, all_three)
    turn(last)
    send(last)
    take(last - 1)
    add_on(0, 3)
    add_on(1, 3)
    pass_on(last - 2)
    take(last)
    pass_on(last - 1)
    add_on(0, 4)
    add_on(1, 4)
    pass_on(last)

    def add_both(s):
        add_on(0, s)
        add_on(1, s)

    each(5, last, add_both)
    add_on(0, last)
    latent_z(1, last - 1).wait_recv()
    latent_z(0, last).wait_recv()
    total_ref[...] = summed[z] + landed[0, last] + landed[1, last - 1]
    ring(0, last).wait_recv()

    def drain(d):
        forward(d, 1).wait_send()
        forward(d, 3).wait_send()
        relay(d, 0).wait()
        relay(d, 1).wait()

    each(0, NZ, drain)

    def drain_rings(s):
        ring(0, s).wait_send()
        ring(1, s).wait_send()
        latent_z(0, s).wait_send()
        latent_z(1, s).wait_send()

    each(0, last, drain_rings)
    ring(0, last).wait_send()
    latent_z(0, last).wait_send()
    each(1, NZ, lambda d: push(d).wait_send())
    cross(1).wait_send()
    cross(3).wait_send()
    for way in range(2):
        cross_out(way).wait_send()
        cross_on(way).wait_send()
    for way in range(2):
        latent_out(way).wait_send()
        latent_on(way).wait_send()
    latent_y(1).wait_send()
    latent_y(3).wait_send()


def exchange(packed, partial):
    whole = pl.BlockSpec(memory_space=pltpu.VMEM)
    wide, lat = partial.shape[1] // NZ, partial.shape[2]
    dma = pltpu.SemaphoreType.DMA
    return pl.pallas_call(
        exchange_kernel,
        out_shape=(
            jax.ShapeDtypeStruct((NY, NZ, 2, CAP, PAD), jnp.bfloat16),
            jax.ShapeDtypeStruct((NZ, 2 * CAP, EXTRA * PAD), jnp.bfloat16),
            jax.ShapeDtypeStruct((wide, lat), jnp.float32),
        ),
        in_specs=[whole] * 2,
        out_specs=(whole,) * 3,
        scratch_shapes=[
            pltpu.VMEM((NY, PARTS, CAP, PAD), jnp.bfloat16),
            pltpu.VMEM((2, PARTS // 2, CAP, PAD), jnp.bfloat16),
            pltpu.VMEM((NZ, 2, CAP, PAD), jnp.bfloat16),
            pltpu.VMEM((2 * CAP, EXTRA * PAD), jnp.bfloat16),
            pltpu.VMEM((NY - 1, NZ * wide, lat), jnp.float32),
            pltpu.VMEM((2, NZ * wide // 2, lat), jnp.float32),
            pltpu.VMEM((NZ, wide, lat), jnp.float32),
            pltpu.VMEM((2, NZ // 2, wide, lat), jnp.float32),
            pltpu.VMEM((2, NZ // 2, wide, lat), jnp.float32),
            dma((3,)),
            dma((2, NZ // 2)),
            dma((2, NZ // 2)),
            dma((NZ,)),
            dma((NZ,)),
            dma((NZ, NY)),
            dma((NZ, NY)),
            dma((2, NZ)),
            dma((2, NZ)),
            dma((NY,)),
            dma((NY,)),
            dma((2, 2)),
            dma((2, 2)),
            dma((2, NZ // 2)),
            dma((2, NZ // 2)),
            dma((NY,)),
            dma((NY,)),
            dma((2, 2)),
            dma((2, 2)),
        ],
        compiler_params=pltpu.CompilerParams(collective_id=0, has_side_effects=True),
        name="exchange",
    )(packed, partial)


def on_device(
    attn_input,
    latent_grad,
    latent_param,
    latent_first,
    latent_second,
    expert_input,
    hidden_grad,
    counts,
    block_owner,
    expert_param,
    expert_first,
    expert_second,
):
    packed = pack(block_owner, counts.T, expert_input[0], hidden_grad[0])
    feat = attn_input.shape[1]
    shard = feat // N_DP
    wide = 16
    source = lax.broadcasted_iota(jnp.int32, (feat, N_DP * wide), 0)
    target = lax.broadcasted_iota(jnp.int32, (feat, N_DP * wide), 1)
    owner = (target // wide % NZ) * NY + target // wide // NZ
    spread = (source == owner * shard + target % wide) & (target % wide < shard)
    columns = jnp.dot(
        attn_input, spread.astype(jnp.bfloat16), preferred_element_type=jnp.bfloat16
    )
    partial = lax.dot_general(
        columns, latent_grad, (((0,), (0,)), ((), ())), preferred_element_type=jnp.float32
    )
    group, hidden, grad_latent = exchange(packed, partial.reshape(NY, NZ * wide, -1))
    group = group.reshape(NY, NZ * 2 * CAP, PAD)
    hidden = hidden.reshape(NZ * 2 * CAP, EXTRA * PAD)
    quarter = jnp.stack(
        [
            lax.dot_general(
                group[i], hidden, (((0,), (0,)), ((), ())), preferred_element_type=jnp.float32
            )[:SHARD]
            for i in range(NY)
        ]
    )
    grad_expert = lax.all_to_all(quarter, "y", split_axis=0, concat_axis=0, tiled=True)
    grad_expert = grad_expert.transpose(1, 0, 2).reshape(1, SHARD, FFE)
    expert_new = adam_step(grad_expert, expert_param, expert_first, expert_second)

    latent_new = adam_step(grad_latent[None, :shard], latent_param, latent_first, latent_second)
    return (*latent_new, *expert_new)


def solution(mesh):
    grid = Mesh(mesh.devices.reshape(NZ, NY, -1), ("z", "y", "expert"))
    dp = ("z", "y")
    sharded = P("expert", dp, None)
    return jax.shard_map(
        on_device,
        mesh=grid,
        in_specs=(
            P(dp, "expert"),
            P(dp, None),
            sharded,
            sharded,
            sharded,
            sharded,
            sharded,
            P(),
            P("expert", None),
            sharded,
            sharded,
            sharded,
        ),
        out_specs=(sharded,) * 6,
        check_vma=False,
    )
```
